256 devices in a mesh: section: 16 (over y, x_lo, core), ep: 16 (over z, x_hi).
Axes of the slice: x: 4 (x_hi: 2, x_lo: 2; x = x_hi * 2 + x_lo), y: 4, z: 8, core: 2. Of those that a mesh axis runs over, the one named last changes fastest.
Arguments:
- grad_out: bfloat16 [16, 8192, 2048], P('section', 'ep'), may hold values from -0.125 to 0.125
- router_weights: bfloat16 [16, 8192, 8], P('section', 'ep'), may hold values from 0.049804688 to 0.29882812
- expert_ids: int32 [16, 8192, 8], P('section', 'ep'), may hold values from 0 to 127, all different within a row; in each aligned block of 512 rows (0 to 511, 512 to 1023, ..., all dimensions but the last counted through in order) at most 64 rows name the same one
- hidden: bfloat16 [16, 16, 768, 1024], P('section', 'ep'), may hold values from -6 to 6
- master: float32 [16, 16, 768, 1024], P('section', 'ep'), may hold values from -0.25 to 0.25
- moment: bfloat16 [16, 16, 768, 1024], P('section', 'ep'), may hold values from -0.049804688 to 0.049804688
- second: bfloat16 [16, 16, 768, 1024], P('section', 'ep'), may hold values from 0.0019989014 to 0.019897461
Outputs:
- update: float32 [16, 16, 768, 1024], P('section', 'ep')
- router_grad: float32 [16, 8192, 8], P('section', 'ep')
The draws below stay inside these ranges and needn't reach their ends.
Inputs may be any that keep to these rules, and one draw needn't show every extreme that they name: `expert_ids`: in the rows of one device (aligned blocks of 512 rows) no expert is named by more than 64 rows, a bound that some block reaches.
All inputs are finite; a program needn't handle non-finite values.
Results may differ from the reference program's by a relative error of at most 0.0029.
Values may be sent and summed in bfloat16 or wider, within the bound.
A program may use at most 128 MiB of HBM per device.

```python
import math
import jax
import jax.numpy as jnp
import numpy as np
from jax import lax

D = 2048
DH = 1024
HID = 768
EXPERTS = 128
TOP = 8
TOK_DEV = 512
CAP = 64
SLOTS = 1024
TOKENS = 8192
N_SECTION = 16
N_EP = 16


def levels(key, shape, shards, low, top_value):
    level = 1.0
    for axis_at, parts in shards:
        heights = jax.random.uniform(jax.random.fold_in(jax.random.fold_in(key, 6), axis_at), (parts,), jnp.float32, low / len(shards), top_value / len(shards))
        level = level * jnp.repeat(jnp.exp(heights), shape[axis_at] // parts).reshape((-1,) + (1,) * (len(shape) - 1 - axis_at))
    return level


def routed_block(key, own, number, rows, count, top, limit, slope):
    ranking = jax.random.permutation(key, count)
    packed, ordinary = portions_of(count, rows * top, limit, slope, True), portions_of(count, rows * top, limit, slope, False)
    places = jnp.arange(count)

    def named(lengths, turn):
        used = int((lengths > 0).sum())
        fixed = max(1, used // 4)
        passed = fixed + (places - fixed + turn * (used - fixed)) % max(1, count - fixed)
        return jnp.zeros((count,), jnp.int32).at[ranking[jnp.where(places < fixed, places, passed)]].set(jnp.asarray(lengths, jnp.int32))

    lengths = jnp.where(number % 4 == 0, named(packed, number // 4), named(ordinary, number - number // 4 - 1))
    mixed = jax.random.permutation(jax.random.fold_in(own, 3), count)
    giver, taker = mixed[0:count // 2 * 2:2], mixed[1:count // 2 * 2:2]
    margin = jnp.minimum(lengths[giver] - 1, limit - lengths[taker]) // 2
    margin = jnp.where((giver == ranking[0]) | (taker == ranking[0]) | (lengths[taker] == 0), 0, jnp.maximum(margin, 0))
    passed = jax.random.randint(jax.random.fold_in(own, 4), (count // 2,), 0, 1 << 20) % (margin + 1)
    lengths = lengths.at[giver].add(-passed).at[taker].add(passed)
    items = jnp.searchsorted(jnp.cumsum(lengths), jnp.arange(rows * top), side="right").astype(jnp.int32)
    listing = items.reshape(top, rows).T
    listing = listing[jax.random.permutation(jax.random.fold_in(own, 1), rows)]
    turn = jax.random.randint(jax.random.fold_in(own, 2), (rows, 1), 0, top)
    return jnp.take_along_axis(listing, (jnp.arange(top)[None, :] + turn) % top, axis=1)


def portions_of(amount, total, bound, slope, full):
    loads = [(1 << 20) // math.isqrt(grade ** slope) + 1 for grade in range(1, amount + 1)]
    largest = bound if full else min(bound, max(-(-total // amount), total * loads[0] // sum(loads)))
    least = 1 if total - largest >= amount - 1 else 0
    given, rest = [largest] + [least] * (amount - 1), total - largest - least * (amount - 1)
    while rest > 0:
        candidates = [i for i in range(1, amount) if given[i] < largest] or [i for i in range(1, amount) if given[i] < bound]
        whole, remaining = sum([loads[i] for i in candidates]), rest
        for i in candidates:
            addition = min(bound - given[i], max(1, remaining * loads[i] // whole), rest)
            given[i] = given[i] + addition
            rest = rest - addition
    return np.array(given)


def noise(key, extent, deviation, reach, pieces=(), kind=jnp.bfloat16):
    result = jax.random.normal(key, extent, jnp.float32) * deviation
    if len(pieces) > 0:
        result = levels(key, extent, pieces, -0.22, 0.18) * result
    return jnp.clip(result, min=-reach, max=reach).astype(kind)


def setup_inputs(seed: int = 0) -> dict:
    arg_keys = jax.random.split(jax.random.key(seed), 8)
    grad_out = noise(arg_keys[0], (N_SECTION, TOKENS, D), (D ** -0.5), 0.125, ((0, 16), (1, 16)))
    router_weights = jnp.clip(0.049804688 + 0.24902344 * jax.random.uniform(arg_keys[1], (N_SECTION, TOKENS, TOP), jnp.float32) ** levels(arg_keys[1], (N_SECTION, TOKENS, TOP), ((0, 16), (1, 16)), -0.2, 0.2), 0.049804688, 0.29882812).astype(jnp.bfloat16)
    expert_ids_keys = jax.random.split(jax.random.fold_in(arg_keys[2], 1), N_SECTION * TOKENS // TOK_DEV)
    expert_ids_turns = jax.random.permutation(jax.random.fold_in(arg_keys[2], 3), N_SECTION * TOKENS // TOK_DEV)
    expert_ids = jax.vmap(lambda own, number: routed_block(jax.random.fold_in(arg_keys[2], 2), own, number, TOK_DEV, EXPERTS, TOP, CAP, 1))(expert_ids_keys, expert_ids_turns).reshape((N_SECTION, TOKENS, TOP))
    hidden = noise(arg_keys[3], (N_SECTION, N_EP, HID, SLOTS), 1.0, 6.0, ((0, 16), (1, 16)))
    master = jnp.clip(jax.random.uniform(arg_keys[4], (N_SECTION, N_EP, HID, DH), jnp.float32, -0.25, 0.25) * levels(arg_keys[4], (N_SECTION, N_EP, HID, DH), ((0, 16), (1, 16)), -0.4, 0.0), -0.25, 0.25)
    moment = jnp.clip(jax.random.uniform(arg_keys[5], (N_SECTION, N_EP, HID, DH), jnp.float32, -0.049804688, 0.049804688) * levels(arg_keys[5], (N_SECTION, N_EP, HID, DH), ((0, 16), (1, 16)), -0.4, 0.0), -0.049804688, 0.049804688).astype(jnp.bfloat16)
    second = jnp.clip(jnp.exp(math.log(0.019897461) - 2.2979944 * jax.random.uniform(arg_keys[6], (N_SECTION, N_EP, HID, DH), jnp.float32) ** levels(arg_keys[6], (N_SECTION, N_EP, HID, DH), ((0, 16), (1, 16)), -0.2, 0.2)), 0.0019989014, 0.019897461).astype(jnp.bfloat16)
    return {"grad_out": grad_out, "router_weights": router_weights, "expert_ids": expert_ids, "hidden": hidden, "master": master, "moment": moment, "second": second}


beta_first = 0.9
beta_second = 0.95
adam_eps = 1e-08
decay_rate = 0.1
first_fix = 1.0 - 0.9 ** 10
second_fix = 1.0 - 0.95 ** 10

def slot_ranks(routes, count):
    onehot = (routes[:, :, None] == jnp.arange(count, dtype=jnp.int32)[None, None, :]).astype(jnp.int32)
    per_token = lax.optimization_barrier(jnp.sum(onehot, axis=1))
    before = jnp.cumsum(per_token, axis=0, dtype=jnp.int32) - per_token
    return lax.optimization_barrier(jnp.sum(before[:, None, :] * onehot, axis=2)).astype(jnp.int32)

def adam_update(total, param, first, second_moment):
    first_new = beta_first * first + (1.0 - beta_first) * total
    second_new = beta_second * second_moment + (1.0 - beta_second) * total * total
    return first_new / first_fix / (jnp.sqrt(second_new / second_fix) + adam_eps) + decay_rate * param

def one_expert(items):
    hid_block, weight, row_block, weight_block = items
    scaled = (hid_block.astype(jnp.float32) * weight_block[None, :].astype(jnp.float32)).astype(jnp.bfloat16)
    grad = jnp.dot(scaled, row_block, preferred_element_type=jnp.float32)
    proj = jnp.einsum('rd,hd->hr', row_block, weight, preferred_element_type=jnp.float32)
    score = lax.optimization_barrier(jnp.sum(hid_block.astype(jnp.float32) * proj, axis=0))
    return (grad, score)

def section_pass(grads_section, weights_section, routes_section, hidden_section, full):
    routes_block = routes_section.reshape(N_EP, TOK_DEV, TOP)
    slots = jax.vmap(lambda block: slot_ranks(block, N_EP))(routes_block)
    source = jnp.arange(N_EP, dtype=jnp.int32)[:, None, None]
    flying = routes_block < N_EP
    flat = jnp.where(flying, (routes_block * N_EP + source) * CAP + slots, N_EP * SLOTS).reshape(-1).astype(jnp.int32)
    token = (source * TOK_DEV + jnp.arange(TOK_DEV, dtype=jnp.int32)[None, :, None] + jnp.zeros_like(routes_block)).reshape(-1)
    rows = jnp.zeros((N_EP * SLOTS, D), grads_section.dtype).at[flat].set(grads_section[token], mode='drop')
    slot_weight = jnp.zeros((N_EP * SLOTS,), weights_section.dtype).at[flat].set(weights_section.reshape(-1), mode='drop')
    grad, score = lax.map(one_expert, (hidden_section, full, rows.reshape(N_EP, SLOTS, D), slot_weight.reshape(N_EP, SLOTS)))
    picked = score.reshape(-1)[jnp.minimum(flat, N_EP * SLOTS - 1)]
    router = jnp.where(flying.reshape(-1), picked, jnp.zeros_like(picked)).reshape(TOKENS, TOP)
    return (grad, router)

def reference(grad_out, router_weights, expert_ids, hidden, master, moment, second):

    def take(array, index):
        return lax.dynamic_index_in_dim(array, index, 0, keepdims=False)

    def pair_pass(low):
        high = (low + N_SECTION // 2).astype(jnp.int32)
        low_master = take(master, low)
        high_master = take(master, high)
        full = jnp.concatenate([low_master, high_master], -1).astype(jnp.bfloat16)
        grad_low, router_low = section_pass(take(grad_out, low), take(router_weights, low), take(expert_ids, low), take(hidden, low), full)
        grad_high, router_high = section_pass(take(grad_out, high), take(router_weights, high), take(expert_ids, high), take(hidden, high), full)
        total_low = grad_low[..., :DH] + grad_high[..., :DH]
        total_high = grad_low[..., DH:] + grad_high[..., DH:]
        up_low = adam_update(total_low, low_master, take(moment, low).astype(jnp.float32), take(second, low).astype(jnp.float32))
        up_high = adam_update(total_high, high_master, take(moment, high).astype(jnp.float32), take(second, high).astype(jnp.float32))
        return (up_low, up_high, router_low, router_high)
    lows, highs, router_lows, router_highs = lax.map(pair_pass, jnp.arange(N_SECTION // 2, dtype=jnp.int32))
    update = jnp.concatenate([lows, highs], 0)
    router = jnp.concatenate([router_lows, router_highs], 0)
    return (update, router)
```

```python
import functools

import jax
import jax.numpy as jnp
from jax import lax
from jax.experimental import pallas as pl
from jax.experimental.pallas import tpu as pltpu
from jax.sharding import PartitionSpec as P

beta_first = 0.9
beta_second = 0.95
adam_eps = 1e-08
decay_rate = 0.1
first_fix = 1.0 - 0.9**10
second_fix = 1.0 - 0.95**10

MESH = pl.DeviceIdType.MESH
F32 = jnp.float32
BF16 = jnp.bfloat16

PIECES = (("far", 0, 512), ("far", 512, 512), ("own", 0, 512), ("own", 512, 512))
ROUTES = tuple(
    (dz, dx) for dz in (4, 3, -3, 2, -2, 1, -1, 0) for dx in (1, 0) if (dz, dx) != (0, 0)
)


def split_three(x):
    high = x.astype(BF16)
    rest = x - high.astype(F32)
    middle = rest.astype(BF16)
    low = (rest - middle.astype(F32)).astype(BF16)
    return high, middle, low


def contract_last(a, b):
    return lax.dot_general(a, b, (((1,), (1,)), ((), ())), preferred_element_type=F32)


def kernel(
    ids_ref, rw_ref, tok_hbm, hid_hbm, mas_hbm, mom_hbm, sec_hbm, upd_hbm, rg_ref,
    toks, sends, recvs, onehot, hid, hid_t, scaled, mas, mom, sec, own_w, far_w, v_buf, acc,
    g_send, g_recv, out, w_send, w_recv, s_send, s_recv,
    tok_sem, in_sem, row_ssem, row_rsem, w_ssem, w_rsem, s_ssem, s_rsem, y_ssem, y_rsem, out_sem,
):
    group, cap = 16, 64
    toks_n = ids_ref.shape[1]
    hid_n, slots = hid.shape
    half = mas.shape[1]
    section = lax.axis_index("section")
    me = lax.axis_index("ep")
    count = lax.axis_size("section")
    mirror = lax.rem(section + count // 2, count)
    lower = (section < count // 2).astype(jnp.int32)
    offsets = {"far": lower * half, "own": (1 - lower) * half}
    z, xh = me // 2, me % 2

    tok_copies = []
    for p, (kind, start, width) in enumerate(PIECES):
        column = pl.multiple_of(offsets[kind] + start, 128)
        tok_copies.append(
            pltpu.make_async_copy(tok_hbm.at[:, pl.ds(column, width)], toks[p], tok_sem.at[p])
        )
    mas_copy = pltpu.make_async_copy(mas_hbm, mas, in_sem.at[0])
    hid_copy = pltpu.make_async_copy(hid_hbm, hid, in_sem.at[1])
    mom_copy = pltpu.make_async_copy(mom_hbm, mom, in_sem.at[2])
    sec_copy = pltpu.make_async_copy(sec_hbm, sec, in_sem.at[3])
    tok_copies[0].start()
    mas_copy.start()
    for copy in tok_copies[1:]:
        copy.start()
    hid_copy.start()
    mom_copy.start()
    sec_copy.start()

    peers = [
        (section, lax.rem(z + dz + 8, 8) * 2 + (lax.rem(xh + dx, 2))) for dz, dx in ROUTES
    ]
    barrier = pltpu.get_barrier_semaphore()
    for peer in peers:
        pl.semaphore_signal(barrier, inc=1, device_id=peer, device_id_type=MESH)
    pl.semaphore_signal(barrier, inc=1, device_id=(mirror, me), device_id_type=MESH)

    ids = ids_ref[...]
    weights = rw_ref[...].astype(F32)
    expert = lax.broadcasted_iota(jnp.int32, (group, toks_n), 0)
    member = jnp.zeros((group, toks_n), F32)
    weight = jnp.zeros((group, toks_n), F32)
    for k in range(ids.shape[0]):
        named = ids[k : k + 1, :] == expert
        member = jnp.where(named, 1.0, member)
        weight = jnp.where(named, weights[k : k + 1, :], weight)
    before = (
        lax.broadcasted_iota(jnp.int32, (toks_n, toks_n), 0)
        < lax.broadcasted_iota(jnp.int32, (toks_n, toks_n), 1)
    )
    rank = jnp.dot(
        member.astype(BF16), before.astype(F32).astype(BF16), preferred_element_type=F32
    ).astype(jnp.int32)
    rank = jnp.where(member > 0.0, rank, -1)
    slot = lax.broadcasted_iota(jnp.int32, (cap, toks_n), 0)
    for e in range(group):
        onehot[e * cap : (e + 1) * cap, :] = jnp.where(
            rank[e : e + 1, :] == slot, 1.0, 0.0
        ).astype(BF16)

    def build(p):
        @pl.loop(0, slots // 256)
        def _(b):
            rows = pl.ds(pl.multiple_of(b * 256, 256), 256)
            sends[p][rows, :] = jnp.dot(
                onehot[rows, :], toks[p][...], preferred_element_type=F32
            ).astype(BF16)

        mine = pl.ds(pl.multiple_of(me * cap, cap), cap)
        recvs[p][mine, :] = sends[p][mine, :]

    def row_copy(p, peer):
        there = pl.ds(pl.multiple_of(peer[1] * cap, cap), cap)
        mine = pl.ds(pl.multiple_of(me * cap, cap), cap)
        return pltpu.make_async_remote_copy(
            src_ref=sends[p].at[there, :],
            dst_ref=recvs[p].at[mine, :],
            send_sem=row_ssem.at[p, peer[1]],
            recv_sem=row_rsem.at[p, me],
            device_id=peer,
            device_id_type=MESH,
        )

    def row_arrival(p, peer):
        there = pl.ds(pl.multiple_of(peer[1] * cap, cap), cap)
        return pltpu.make_async_remote_copy(
            src_ref=sends[p].at[there, :],
            dst_ref=recvs[p].at[there, :],
            send_sem=row_ssem.at[p, peer[1]],
            recv_sem=row_rsem.at[p, peer[1]],
            device_id=peer,
            device_id_type=MESH,
        )

    tok_copies[0].wait()
    build(0)
    pl.semaphore_wait(barrier, len(peers) + 1)
    for peer in peers:
        row_copy(0, peer).start()

    spread = contract_last(weight.astype(BF16), onehot[...])
    row = lax.broadcasted_iota(jnp.int32, (group, 128), 0)
    lane = lax.broadcasted_iota(jnp.int32, (group, 128), 1)
    packed = jnp.zeros((group, 128), F32)
    for q in range(slots // 128):
        packed = jnp.where(row // 2 == q, spread[:, q * 128 : (q + 1) * 128], packed)
    packed = jnp.where(lane // cap == row % 2, packed, 0.0)
    packed = packed + pltpu.roll(packed, cap, 1)
    for e in range(group):
        w_send[e] = jnp.broadcast_to(packed[e : e + 1, :], (8, 128))
    w_recv[me] = w_send[me]

    def small_copy(source, target, ssem, rsem, at, peer):
        return pltpu.make_async_remote_copy(
            src_ref=source.at[at],
            dst_ref=target.at[me],
            send_sem=ssem.at[peer[1]],
            recv_sem=rsem.at[me],
            device_id=peer,
            device_id_type=MESH,
        )

    def small_arrival(source, target, ssem, rsem, peer):
        return pltpu.make_async_remote_copy(
            src_ref=source.at[0],
            dst_ref=target.at[peer[1]],
            send_sem=ssem.at[peer[1]],
            recv_sem=rsem.at[peer[1]],
            device_id=peer,
            device_id_type=MESH,
        )

    for peer in peers:
        small_copy(w_send, w_recv, w_ssem, w_rsem, peer[1], peer).start()

    mas_copy.wait()
    own_w[...] = mas[...].astype(BF16)
    far_copy = pltpu.make_async_remote_copy(
        src_ref=own_w, dst_ref=far_w, send_sem=y_ssem.at[0], recv_sem=y_rsem.at[0],
        device_id=(mirror, me), device_id_type=MESH,
    )
    far_copy.start()

    for p in range(1, len(PIECES)):
        tok_copies[p].wait()
        build(p)
        for peer in peers:
            row_copy(p, peer).start()

    hid_copy.wait()

    @pl.loop(0, slots // 256)
    def _(b):
        rows = pl.ds(pl.multiple_of(b * 256, 256), 256)
        hid_t[rows, :] = hid[:, rows].T

    for peer in peers:
        small_arrival(w_send, w_recv, w_ssem, w_rsem, peer).wait_recv()
    lane8 = lax.broadcasted_iota(jnp.int32, (8, 128), 1)
    slot_w = jnp.concatenate(
        [jnp.where(lane8 < cap, w_recv[2 * q], w_recv[2 * q + 1]) for q in range(slots // 128)], 1
    )[0:1, :]

    @pl.loop(0, hid_n // 64)
    def _(b):
        rows = pl.ds(pl.multiple_of(b * 64, 64), 64)
        scaled[rows, :] = (hid[rows, :].astype(F32) * slot_w).astype(BF16)

    def project(p):
        kind, start, width = PIECES[p]
        matrix = own_w if kind == "own" else far_w
        base = start + (half if kind == "own" else 0)

        @pl.loop(0, slots // 256)
        def _(b):
            rows = pl.ds(pl.multiple_of(b * 256, 256), 256)
            v_buf[rows, base : base + width] = jnp.dot(
                hid_t[rows, :], matrix[:, start : start + width], preferred_element_type=F32
            )

    def add_score(p, first):
        kind, start, width = PIECES[p]
        base = start + (half if kind == "own" else 0)

        @pl.loop(0, slots // 64)
        def _(b):
            rows = pl.ds(pl.multiple_of(b * 64, 64), 64)
            product = recvs[p][rows, :].astype(F32) * v_buf[rows, base : base + width]
            partial = product[:, 0:128]
            for q in range(1, width // 128):
                partial = partial + product[:, q * 128 : (q + 1) * 128]
            if first:
                acc[rows, :] = partial
            else:
                acc[rows, :] = acc[rows, :] + partial

    def await_rows(p):
        for peer in peers:
            row_arrival(p, peer).wait_recv()

    def grad_copy(p):
        kind, start, width = PIECES[p]
        return pltpu.make_async_remote_copy(
            src_ref=g_send.at[:, pl.ds(start, width)],
            dst_ref=g_recv.at[:, pl.ds(start, width)],
            send_sem=y_ssem.at[1 + p],
            recv_sem=y_rsem.at[1 + p],
            device_id=(mirror, me),
            device_id_type=MESH,
        )

    far = [p for p, piece in enumerate(PIECES) if piece[0] == "far"]
    own = [p for p, piece in enumerate(PIECES) if piece[0] == "own"]
    for p in own:
        project(p)
    for n, p in enumerate(far):
        kind, start, width = PIECES[p]
        await_rows(p)

        @pl.loop(0, hid_n // 256)
        def _(b):
            rows = pl.ds(pl.multiple_of(b * 256, 256), 256)
            g_send[rows, start : start + width] = jnp.dot(
                scaled[rows, :], recvs[p][...], preferred_element_type=F32
            ).astype(BF16)

        grad_copy(p).start()
        if n == 0:
            far_copy.wait_recv()
        project(p)
        add_score(p, n == 0)

    mom_copy.wait()
    sec_copy.wait()

    def finish(p):
        kind, start, width = PIECES[p]

        @pl.loop(0, hid_n // 128)
        def _(b):
            rows = pl.ds(pl.multiple_of(b * 128, 128), 128)
            cols = slice(start, start + width)
            total = (
                jnp.dot(scaled[rows, :], recvs[p][...], preferred_element_type=F32)
                + g_recv[rows, cols].astype(F32)
            )
            first_new = beta_first * mom[rows, cols].astype(F32) + (1.0 - beta_first) * total
            second_new = (
                beta_second * sec[rows, cols].astype(F32) + (1.0 - beta_second) * total * total
            )
            out[rows, cols] = (
                first_new / first_fix / (jnp.sqrt(second_new / second_fix) + adam_eps)
                + decay_rate * mas[rows, cols]
            )

        copy = pltpu.make_async_copy(
            out.at[:, pl.ds(start, width)], upd_hbm.at[:, pl.ds(start, width)], out_sem.at[p]
        )
        copy.start()
        return copy

    out_copies = []
    for p in own[:-1]:
        await_rows(p)
        add_score(p, False)
        for q in far:
            if PIECES[q][1] == PIECES[p][1]:
                grad_copy(q).wait_recv()
        out_copies.append(finish(p))

    last = own[-1]
    await_rows(last)
    add_score(last, False)
    ones = jnp.ones((8, 128), BF16)
    score = jnp.zeros((8, slots), F32)
    for part in split_three(acc[...]):
        score = score + contract_last(ones, part)
    for q in range(slots // 128):
        s_send[q] = score[:, q * 128 : (q + 1) * 128]
    s_recv[me] = s_send[me // 2]
    for peer in peers:
        small_copy(s_send, s_recv, s_ssem, s_rsem, peer[1] // 2, peer).start()
    for q in far:
        if PIECES[q][1] == PIECES[last][1]:
            grad_copy(q).wait_recv()
    out_copies.append(finish(last))

    for peer in peers:
        small_arrival(s_send, s_recv, s_ssem, s_rsem, peer).wait_recv()
    got = jnp.concatenate([s_recv[e][0:1, :] for e in range(group)], 0)
    mine = lane // cap == xh
    got = jnp.where(mine, got, pltpu.roll(got, cap, 1))
    wide_row = lax.broadcasted_iota(jnp.int32, (group, slots), 0)
    wide_lane = lax.broadcasted_iota(jnp.int32, (group, slots), 1)
    wide = jnp.where(wide_lane // cap == wide_row, jnp.concatenate([got] * (slots // 128), 1), 0.0)
    found = jnp.zeros((group, toks_n), F32)
    for part in split_three(wide):
        found = found + jnp.dot(part, onehot[...], preferred_element_type=F32)
    for k in range(ids.shape[0]):
        rg_ref[k : k + 1, :] = jnp.sum(
            jnp.where(ids[k : k + 1, :] == expert, found, 0.0), axis=0, keepdims=True
        )

    for copy in out_copies:
        copy.wait()
    far_copy.wait_send()
    for p in far:
        grad_copy(p).wait_send()
    for peer in peers:
        for p in range(len(PIECES)):
            row_copy(p, peer).wait_send()
        small_copy(w_send, w_recv, w_ssem, w_rsem, peer[1], peer).wait_send()
        small_copy(s_send, s_recv, s_ssem, s_rsem, peer[1] // 2, peer).wait_send()


def local(grad_out, router_weights, expert_ids, hidden, master, moment, second):
    toks_n, width = grad_out.shape[1:]
    hid_n, slots = hidden.shape[2:]
    half = master.shape[3]
    top = expert_ids.shape[2]
    pieces = len(PIECES)
    dma = pltpu.SemaphoreType.DMA
    hbm = pl.BlockSpec(memory_space=pl.ANY)
    vmem = pl.BlockSpec(memory_space=pltpu.VMEM)
    update, router = pl.pallas_call(
        kernel,
        out_shape=(
            jax.ShapeDtypeStruct((hid_n, half), F32),
            jax.ShapeDtypeStruct((top, toks_n), F32),
        ),
        in_specs=[vmem, vmem, hbm, hbm, hbm, hbm, hbm],
        out_specs=(hbm, vmem),
        scratch_shapes=[
            [pltpu.VMEM((toks_n, w), BF16) for _, _, w in PIECES],
            [pltpu.VMEM((slots, w), BF16) for _, _, w in PIECES],
            [pltpu.VMEM((slots, w), BF16) for _, _, w in PIECES],
            pltpu.VMEM((slots, toks_n), BF16),
            pltpu.VMEM((hid_n, slots), BF16),
            pltpu.VMEM((slots, hid_n), BF16),
            pltpu.VMEM((hid_n, slots), BF16),
            pltpu.VMEM((hid_n, half), F32),
            pltpu.VMEM((hid_n, half), BF16),
            pltpu.VMEM((hid_n, half), BF16),
            pltpu.VMEM((hid_n, half), BF16),
            pltpu.VMEM((hid_n, half), BF16),
            pltpu.VMEM((slots, width), F32),
            pltpu.VMEM((slots, 128), F32),
            pltpu.VMEM((hid_n, half), BF16),
            pltpu.VMEM((hid_n, half), BF16),
            pltpu.VMEM((hid_n, half), F32),
            pltpu.VMEM((16, 8, 128), F32),
            pltpu.VMEM((16, 8, 128), F32),
            pltpu.VMEM((8, 8, 128), F32),
            pltpu.VMEM((16, 8, 128), F32),
            dma((pieces,)),
            dma((4,)),
            dma((pieces, 16)),
            dma((pieces, 16)),
            dma((16,)),
            dma((16,)),
            dma((16,)),
            dma((16,)),
            dma((1 + pieces,)),
            dma((1 + pieces,)),
            dma((pieces,)),
        ],
        compiler_params=pltpu.CompilerParams(
            collective_id=0, has_side_effects=True, vmem_limit_bytes=56 << 20
        ),
    )(
        expert_ids[0].T, router_weights[0].T, grad_out[0], hidden[0, 0], master[0, 0],
        moment[0, 0], second[0, 0],
    )
    return (update[None, None], router.T[None])


def solution(mesh):
    placed = (
        P("section", "ep", None),
        P("section", "ep", None),
        P("section", "ep", None),
        P("section", "ep", None, None),
        P("section", "ep", None, None),
        P("section", "ep", None, None),
        P("section", "ep", None, None),
    )
    return jax.shard_map(
        local,
        mesh=mesh,
        in_specs=placed,
        out_specs=(P("section", "ep", None, None), P("section", "ep", None)),
        check_vma=False,
    )
```

```python
import functools

import jax
import jax.numpy as jnp
from jax import lax
from jax.experimental import pallas as pl
from jax.experimental.pallas import tpu as pltpu
from jax.sharding import PartitionSpec as P

beta_first = 0.9
beta_second = 0.95
adam_eps = 1e-08
decay_rate = 0.1
first_fix = 1.0 - 0.9**10
second_fix = 1.0 - 0.95**10

MESH = pl.DeviceIdType.MESH
F32 = jnp.float32
BF16 = jnp.bfloat16

PIECES = (("far", 0, 256), ("far", 256, 768), ("own", 0, 512), ("own", 512, 384), ("own", 896, 128))
ROUTES = tuple(
    (dz, dx) for dz in (0, -1, 1, -2, 2, -3, 3, 4) for dx in (0, 1) if (dz, dx) != (0, 0)
)


def split_two(x):
    high = x.astype(BF16)
    return high, (x - high.astype(F32)).astype(BF16)


def blocks(start, width):
    return [(c, min(256, start + width - c)) for c in range(start, start + width, 256)]


def contract_last(a, b):
    return lax.dot_general(a, b, (((1,), (1,)), ((), ())), preferred_element_type=F32)


def kernel(
    ids_ref, rw_ref, tok_hbm, hid_hbm, mas_hbm, mom_hbm, sec_hbm, out, rg_ref,
    toks, sends, recvs, onehot, hid, hid_t, scaled, mas, mom, sec, own_w, far_w, v_buf, acc,
    g_send, g_recv, fresh, w_send, w_recv, s_send, s_recv,
    tok_sem, in_sem, row_ssem, row_rsem, w_sem, s_sem, y_ssem, y_rsem,
):
    group, cap = 16, 64
    toks_n = ids_ref.shape[1]
    hid_n, slots = hid.shape
    half = mas.shape[1]
    section = lax.axis_index("section")
    me = lax.axis_index("ep")
    count = lax.axis_size("section")
    mirror = lax.rem(section + count // 2, count)
    lower = (section < count // 2).astype(jnp.int32)
    offsets = {"far": lower * half, "own": (1 - lower) * half}
    z, xh = me // 2, me % 2

    tok_copies = []
    for p, (kind, start, width) in enumerate(PIECES):
        column = pl.multiple_of(offsets[kind] + start, 128)
        tok_copies.append(
            pltpu.make_async_copy(tok_hbm.at[:, pl.ds(column, width)], toks[p], tok_sem.at[p])
        )
    mas_copy = pltpu.make_async_copy(mas_hbm, mas, in_sem.at[0])
    hid_copy = pltpu.make_async_copy(hid_hbm, hid, in_sem.at[1])
    mom_copy = pltpu.make_async_copy(mom_hbm, mom, in_sem.at[2])
    sec_copy = pltpu.make_async_copy(sec_hbm, sec, in_sem.at[3])
    tok_copies[0].start()
    mas_copy.start()
    for copy in tok_copies[1:]:
        copy.start()
    hid_copy.start()
    mom_copy.start()
    sec_copy.start()

    peers = [
        (section, lax.rem(z + dz + 8, 8) * 2 + (lax.rem(xh + dx, 2))) for dz, dx in ROUTES
    ]
    barrier = pltpu.get_barrier_semaphore()
    for peer in peers:
        pl.semaphore_signal(barrier, inc=1, device_id=peer, device_id_type=MESH)
    pl.semaphore_signal(barrier, inc=1, device_id=(mirror, me), device_id_type=MESH)

    ids = ids_ref[...]
    weights = rw_ref[...].astype(F32)
    expert = lax.broadcasted_iota(jnp.int32, (group, toks_n), 0)
    member = jnp.zeros((group, toks_n), F32)
    weight = jnp.zeros((group, toks_n), F32)
    for k in range(ids.shape[0]):
        named = ids[k : k + 1, :] == expert
        member = jnp.where(named, 1.0, member)
        weight = jnp.where(named, weights[k : k + 1, :], weight)
    parts = [member[:, b * 128 : (b + 1) * 128] for b in range(toks_n // 128)]
    column = lax.broadcasted_iota(jnp.int32, (128, 256), 1)
    before = (lax.broadcasted_iota(jnp.int32, (128, 256), 0) < column) | (column >= 128)
    counted = jnp.dot(
        jnp.concatenate(parts, 0).astype(BF16),
        jnp.where(before, 1.0, 0.0).astype(BF16),
        preferred_element_type=F32,
    )
    passed = jnp.zeros((group, 128), F32)
    ranks = []
    for b in range(toks_n // 128):
        rows = slice(b * group, (b + 1) * group)
        ranks.append(counted[rows, :128] + passed)
        passed = passed + counted[rows, 128:]
    rank = jnp.concatenate(ranks, 1).astype(jnp.int32)
    rank = jnp.where(member > 0.0, rank, -1)
    slot = lax.broadcasted_iota(jnp.int32, (cap, toks_n), 0)
    for e in range(group):
        onehot[e * cap : (e + 1) * cap, :] = jnp.where(
            rank[e : e + 1, :] == slot, 1.0, 0.0
        ).astype(BF16)

    def build(p):
        @pl.loop(0, slots // 256)
        def _(b):
            rows = pl.ds(pl.multiple_of(b * 256, 256), 256)
            sends[p][rows, :] = jnp.dot(
                onehot[rows, :], toks[p][...], preferred_element_type=F32
            ).astype(BF16)

        mine = pl.ds(pl.multiple_of(me * cap, cap), cap)
        recvs[p][mine, :] = sends[p][mine, :]

    def row_copy(p, peer):
        there = pl.ds(pl.multiple_of(peer[1] * cap, cap), cap)
        mine = pl.ds(pl.multiple_of(me * cap, cap), cap)
        return pltpu.make_async_remote_copy(
            src_ref=sends[p].at[there, :],
            dst_ref=recvs[p].at[mine, :],
            send_sem=row_ssem.at[p],
            recv_sem=row_rsem.at[p],
            device_id=peer,
            device_id_type=MESH,
        )

    def all_rows(p):
        rows = pl.ds(0, len(peers) * cap)
        return pltpu.make_async_remote_copy(
            src_ref=sends[p].at[rows, :],
            dst_ref=recvs[p].at[rows, :],
            send_sem=row_ssem.at[p],
            recv_sem=row_rsem.at[p],
            device_id=peers[0],
            device_id_type=MESH,
        )

    tok_copies[0].wait()
    build(0)
    pl.semaphore_wait(barrier, len(peers) + 1)
    for peer in peers:
        row_copy(0, peer).start()

    spread = contract_last(weight.astype(BF16), onehot[...])
    row = lax.broadcasted_iota(jnp.int32, (group, 128), 0)
    lane = lax.broadcasted_iota(jnp.int32, (group, 128), 1)
    packed = jnp.zeros((group, 128), F32)
    for q in range(slots // 128):
        packed = jnp.where(row // 2 == q, spread[:, q * 128 : (q + 1) * 128], packed)
    packed = jnp.where(lane // cap == row % 2, packed, 0.0)
    packed = packed + pltpu.roll(packed, cap, 1)
    for e in range(group):
        w_send[e] = jnp.broadcast_to(packed[e : e + 1, :], (8, 128))
    w_recv[me] = w_send[me]

    def small_copy(source, target, sems, at, peer):
        return pltpu.make_async_remote_copy(
            src_ref=source.at[at],
            dst_ref=target.at[me],
            send_sem=sems.at[0],
            recv_sem=sems.at[1],
            device_id=peer,
            device_id_type=MESH,
        )

    def all_small(target, sems):
        return pltpu.make_async_remote_copy(
            src_ref=target.at[pl.ds(0, len(peers))],
            dst_ref=target.at[pl.ds(0, len(peers))],
            send_sem=sems.at[0],
            recv_sem=sems.at[1],
            device_id=peers[0],
            device_id_type=MESH,
        )

    for peer in peers:
        small_copy(w_send, w_recv, w_sem, peer[1], peer).start()

    mas_copy.wait()
    own_w[...] = mas[...].astype(BF16)
    far_copy = pltpu.make_async_remote_copy(
        src_ref=own_w, dst_ref=far_w, send_sem=y_ssem.at[0], recv_sem=y_rsem.at[0],
        device_id=(mirror, me), device_id_type=MESH,
    )
    far_copy.start()

    for p in range(1, len(PIECES)):
        tok_copies[p].wait()
        build(p)
        for peer in peers:
            row_copy(p, peer).start()

    hid_copy.wait()

    @pl.loop(0, slots // 256)
    def _(b):
        rows = pl.ds(pl.multiple_of(b * 256, 256), 256)
        hid_t[rows, :] = hid[:, rows].T

    all_small(w_recv, w_sem).wait_recv()
    lane8 = lax.broadcasted_iota(jnp.int32, (8, 128), 1)
    slot_w = jnp.concatenate(
        [jnp.where(lane8 < cap, w_recv[2 * q], w_recv[2 * q + 1]) for q in range(slots // 128)], 1
    )[0:1, :]

    @pl.loop(0, hid_n // 64)
    def _(b):
        rows = pl.ds(pl.multiple_of(b * 64, 64), 64)
        scaled[rows, :] = (hid[rows, :].astype(F32) * slot_w).astype(BF16)

    def project(p):
        kind, start, width = PIECES[p]
        matrix = own_w if kind == "own" else far_w
        base = start + (half if kind == "own" else 0)

        @pl.loop(0, slots // 256)
        def _(b):
            rows = pl.ds(pl.multiple_of(b * 256, 256), 256)
            v_buf[rows, base : base + width] = jnp.dot(
                hid_t[rows, :], matrix[:, start : start + width], preferred_element_type=F32
            )

    def add_score(p, first):
        kind, start, width = PIECES[p]
        base = start + (half if kind == "own" else 0)

        @pl.loop(0, slots // 64)
        def _(b):
            rows = pl.ds(pl.multiple_of(b * 64, 64), 64)
            product = recvs[p][rows, :].astype(F32) * v_buf[rows, base : base + width]
            partial = product[:, 0:128]
            for q in range(1, width // 128):
                partial = partial + product[:, q * 128 : (q + 1) * 128]
            if first:
                acc[rows, :] = partial
            else:
                acc[rows, :] = acc[rows, :] + partial

    def await_rows(p):
        all_rows(p).wait_recv()

    def grad_copy(p):
        kind, start, width = PIECES[p]
        return pltpu.make_async_remote_copy(
            src_ref=g_send.at[:, pl.ds(start, width)],
            dst_ref=g_recv.at[:, pl.ds(start, width)],
            send_sem=y_ssem.at[1 + p],
            recv_sem=y_rsem.at[1 + p],
            device_id=(mirror, me),
            device_id_type=MESH,
        )

    far = [p for p, piece in enumerate(PIECES) if piece[0] == "far"]
    own = [p for p, piece in enumerate(PIECES) if piece[0] == "own"]
    for p in own:
        project(p)
    for n, p in enumerate(far):
        kind, start, width = PIECES[p]
        await_rows(p)

        @pl.loop(0, hid_n // 256)
        def _(b):
            rows = pl.ds(pl.multiple_of(b * 256, 256), 256)
            g_send[rows, start : start + width] = jnp.dot(
                scaled[rows, :], recvs[p][...], preferred_element_type=F32
            ).astype(BF16)

        grad_copy(p).start()
        if n == 0:
            far_copy.wait_recv()
        project(p)
        add_score(p, n == 0)

    mom_copy.wait()
    sec_copy.wait()

    arrived = []

    def finish(p):
        kind, start, width = PIECES[p]
        for q in far:
            if q not in arrived and PIECES[q][1] < start + width:
                grad_copy(q).wait_recv()
                arrived.append(q)
        for c, n in blocks(0, width):
            fresh[:, :n] = jnp.dot(
                scaled[...], recvs[p][:, c : c + n], preferred_element_type=F32
            )

            @pl.loop(0, hid_n // 64)
            def _(b):
                rows = pl.ds(pl.multiple_of(b * 64, 64), 64)
                cols = slice(start + c, start + c + n)
                total = fresh[rows, :n] + g_recv[rows, cols].astype(F32)
                first_new = (beta_first / first_fix) * mom[rows, cols].astype(F32) + (
                    (1.0 - beta_first) / first_fix
                ) * total
                second_new = (beta_second / second_fix) * sec[rows, cols].astype(F32) + (
                    (1.0 - beta_second) / second_fix
                ) * (total * total)
                out[rows, cols] = (
                    first_new / (jnp.sqrt(second_new) + adam_eps) + decay_rate * mas[rows, cols]
                )

    for p in own[:-1]:
        await_rows(p)
        add_score(p, False)
        finish(p)

    last = own[-1]
    await_rows(last)
    add_score(last, False)
    score = contract_last(jnp.ones((8, 256), BF16), jnp.concatenate(split_two(acc[...]), 1))
    for q in range(slots // 128):
        s_send[q] = score[:, q * 128 : (q + 1) * 128]
    s_recv[me] = s_send[me // 2]
    for peer in peers:
        small_copy(s_send, s_recv, s_sem, peer[1] // 2, peer).start()
    finish(last)

    all_small(s_recv, s_sem).wait_recv()
    got = jnp.concatenate([s_recv[e][0:1, :] for e in range(group)], 0)
    mine = lane // cap == xh
    got = jnp.where(mine, got, pltpu.roll(got, cap, 1))
    found = jnp.concatenate(
        [
            jnp.take_along_axis(got, jnp.maximum(rank[:, b * 128 : (b + 1) * 128], 0), axis=1)
            for b in range(toks_n // 128)
        ],
        1,
    )
    for k in range(ids.shape[0]):
        rg_ref[k : k + 1, :] = jnp.sum(
            jnp.where(ids[k : k + 1, :] == expert, found, 0.0), axis=0, keepdims=True
        )

    far_copy.wait_send()
    for p in far:
        grad_copy(p).wait_send()
    for p in range(len(PIECES)):
        all_rows(p).wait_send()
    all_small(w_recv, w_sem).wait_send()
    all_small(s_recv, s_sem).wait_send()


def local(grad_out, router_weights, expert_ids, hidden, master, moment, second):
    toks_n, width = grad_out.shape[1:]
    hid_n, slots = hidden.shape[2:]
    half = master.shape[3]
    top = expert_ids.shape[2]
    pieces = len(PIECES)
    dma = pltpu.SemaphoreType.DMA
    hbm = pl.BlockSpec(memory_space=pl.ANY)
    vmem = pl.BlockSpec(memory_space=pltpu.VMEM)
    update, router = pl.pallas_call(
        kernel,
        out_shape=(
            pltpu.VMEM((hid_n, half), F32),
            pltpu.VMEM((top, toks_n), F32),
        ),
        in_specs=[vmem, vmem, hbm, hbm, hbm, hbm, hbm],
        out_specs=(vmem, vmem),
        scratch_shapes=[
            [pltpu.VMEM((toks_n, w), BF16) for _, _, w in PIECES],
            [pltpu.VMEM((slots, w), BF16) for _, _, w in PIECES],
            [pltpu.VMEM((slots, w), BF16) for _, _, w in PIECES],
            pltpu.VMEM((slots, toks_n), BF16),
            pltpu.VMEM((hid_n, slots), BF16),
            pltpu.VMEM((slots, hid_n), BF16),
            pltpu.VMEM((hid_n, slots), BF16),
            pltpu.VMEM((hid_n, half), F32),
            pltpu.VMEM((hid_n, half), BF16),
            pltpu.VMEM((hid_n, half), BF16),
            pltpu.VMEM((hid_n, half), BF16),
            pltpu.VMEM((hid_n, half), BF16),
            pltpu.VMEM((slots, width), F32),
            pltpu.VMEM((slots, 128), F32),
            pltpu.VMEM((hid_n, half), BF16),
            pltpu.VMEM((hid_n, half), BF16),
            pltpu.VMEM((hid_n, 256), F32),
            pltpu.VMEM((16, 8, 128), F32),
            pltpu.VMEM((16, 8, 128), F32),
            pltpu.VMEM((8, 8, 128), F32),
            pltpu.VMEM((16, 8, 128), F32),
            dma((pieces,)),
            dma((4,)),
            dma((pieces,)),
            dma((pieces,)),
            dma((2,)),
            dma((2,)),
            dma((1 + pieces,)),
            dma((1 + pieces,)),
        ],
        compiler_params=pltpu.CompilerParams(
            collective_id=0, has_side_effects=True, vmem_limit_bytes=58 << 20
        ),
    )(
        expert_ids[0].T, router_weights[0].T, grad_out[0], hidden[0, 0], master[0, 0],
        moment[0, 0], second[0, 0],
    )
    return (update[None, None], router.T[None])


def solution(mesh):
    placed = (
        P("section", "ep", None),
        P("section", "ep", None),
        P("section", "ep", None),
        P("section", "ep", None, None),
        P("section", "ep", None, None),
        P("section", "ep", None, None),
        P("section", "ep", None, None),
    )
    return jax.shard_map(
        local,
        mesh=mesh,
        in_specs=placed,
        out_specs=(P("section", "ep", None, None), P("section", "ep", None)),
        check_vma=False,
    )
```

```python
import functools

import jax
import jax.numpy as jnp
from jax import lax
from jax.experimental import pallas as pl
from jax.experimental.pallas import tpu as pltpu
from jax.sharding import PartitionSpec as P

beta_first = 0.9
beta_second = 0.95
adam_eps = 1e-08
decay_rate = 0.1
first_fix = 1.0 - 0.9**10
second_fix = 1.0 - 0.95**10

MESH = pl.DeviceIdType.MESH
F32 = jnp.float32
BF16 = jnp.bfloat16

PIECES = (("far", 0, 512), ("far", 512, 512), ("own", 0, 512), ("own", 512, 256), ("own", 768, 256))
GROUPS = ((4, 3, -3), (2, -2), (1, -1, 0))
ROUTES = tuple(
    (dz, dx) for dz in (4, 3, -3, 2, -2, 1, -1, 0) for dx in (0, 1) if (dz, dx) != (0, 0)
)


def split_two(x):
    high = x.astype(BF16)
    return high, (x - high.astype(F32)).astype(BF16)


def blocks(start, width):
    return [(c, min(256, start + width - c)) for c in range(start, start + width, 256)]


def contract_last(a, b):
    return lax.dot_general(a, b, (((1,), (1,)), ((), ())), preferred_element_type=F32)


def kernel(
    ids_ref, rw_ref, tok_hbm, hid_hbm, mas_hbm, mom_hbm, sec_hbm, out, rg_ref,
    toks, sends, recvs, onehot, hid, hid_t, scaled, mas, mom, sec, own_w, far_w, v_buf, acc,
    g_send, g_recv, fresh, w_send, w_recv, s_send, s_recv,
    tok_sem, in_sem, row_ssem, row_rsem, w_sem, s_sem, y_ssem, y_rsem,
):
    group, cap = 16, 64
    toks_n = ids_ref.shape[1]
    hid_n, slots = hid.shape
    half = mas.shape[1]
    section = lax.axis_index("section")
    me = lax.axis_index("ep")
    count = lax.axis_size("section")
    mirror = lax.rem(section + count // 2, count)
    lower = (section < count // 2).astype(jnp.int32)
    offsets = {"far": lower * half, "own": (1 - lower) * half}
    z, xh = me // 2, me % 2

    tok_copies = []
    for p, (kind, start, width) in enumerate(PIECES):
        column = pl.multiple_of(offsets[kind] + start, 128)
        tok_copies.append(
            pltpu.make_async_copy(tok_hbm.at[:, pl.ds(column, width)], toks[p], tok_sem.at[p])
        )
    mas_copy = pltpu.make_async_copy(mas_hbm, mas, in_sem.at[0])
    hid_copy = pltpu.make_async_copy(hid_hbm, hid, in_sem.at[1])
    mom_copy = pltpu.make_async_copy(mom_hbm, mom, in_sem.at[2])
    sec_copy = pltpu.make_async_copy(sec_hbm, sec, in_sem.at[3])
    tok_copies[0].start()
    mas_copy.start()
    for copy in tok_copies[1:]:
        copy.start()
    hid_copy.start()
    mom_copy.start()
    sec_copy.start()

    peers = [
        (section, lax.rem(z + dz + 8, 8) * 2 + (lax.rem(xh + dx, 2))) for dz, dx in ROUTES
    ]
    bands = [
        [peer for (dz, _), peer in zip(ROUTES, peers) if dz in group_dz] for group_dz in GROUPS
    ]
    barrier = pltpu.get_barrier_semaphore()
    for peer in peers:
        pl.semaphore_signal(barrier, inc=1, device_id=peer, device_id_type=MESH)
    pl.semaphore_signal(barrier, inc=1, device_id=(mirror, me), device_id_type=MESH)

    ids = ids_ref[...]
    weights = rw_ref[...].astype(F32)
    expert = lax.broadcasted_iota(jnp.int32, (group, toks_n), 0)
    member = jnp.zeros((group, toks_n), F32)
    weight = jnp.zeros((group, toks_n), F32)
    for k in range(ids.shape[0]):
        named = ids[k : k + 1, :] == expert
        member = jnp.where(named, 1.0, member)
        weight = jnp.where(named, weights[k : k + 1, :], weight)
    parts = [member[:, b * 128 : (b + 1) * 128] for b in range(toks_n // 128)]
    column = lax.broadcasted_iota(jnp.int32, (128, 256), 1)
    before = (lax.broadcasted_iota(jnp.int32, (128, 256), 0) < column) | (column >= 128)
    counted = jnp.dot(
        jnp.concatenate(parts, 0).astype(BF16),
        jnp.where(before, 1.0, 0.0).astype(BF16),
        preferred_element_type=F32,
    )
    passed = jnp.zeros((group, 128), F32)
    ranks = []
    for b in range(toks_n // 128):
        rows = slice(b * group, (b + 1) * group)
        ranks.append(counted[rows, :128] + passed)
        passed = passed + counted[rows, 128:]
    rank = jnp.concatenate(ranks, 1).astype(jnp.int32)
    rank = jnp.where(member > 0.0, rank, -1)
    slot = lax.broadcasted_iota(jnp.int32, (cap, toks_n), 0)
    for e in range(group):
        onehot[e * cap : (e + 1) * cap, :] = jnp.where(
            rank[e : e + 1, :] == slot, 1.0, 0.0
        ).astype(BF16)

    def build(p):
        @pl.loop(0, slots // 256)
        def _(b):
            rows = pl.ds(pl.multiple_of(b * 256, 256), 256)
            sends[p][rows, :] = jnp.dot(
                onehot[rows, :], toks[p][...], preferred_element_type=F32
            ).astype(BF16)

        mine = pl.ds(pl.multiple_of(me * cap, cap), cap)
        recvs[p][mine, :] = sends[p][mine, :]

    def row_copy(p, peer, sem=None):
        sem = p if sem is None else sem
        there = pl.ds(pl.multiple_of(peer[1] * cap, cap), cap)
        mine = pl.ds(pl.multiple_of(me * cap, cap), cap)
        return pltpu.make_async_remote_copy(
            src_ref=sends[p].at[there, :],
            dst_ref=recvs[p].at[mine, :],
            send_sem=row_ssem.at[sem],
            recv_sem=row_rsem.at[sem],
            device_id=peer,
            device_id_type=MESH,
        )

    def all_rows(p, sem=None, number=None):
        sem = p if sem is None else sem
        rows = pl.ds(0, (len(peers) if number is None else number) * cap)
        return pltpu.make_async_remote_copy(
            src_ref=sends[p].at[rows, :],
            dst_ref=recvs[p].at[rows, :],
            send_sem=row_ssem.at[sem],
            recv_sem=row_rsem.at[sem],
            device_id=peers[0],
            device_id_type=MESH,
        )

    tok_copies[0].wait()
    build(0)
    pl.semaphore_wait(barrier, len(peers) + 1)
    for peer in peers:
        row_copy(0, peer).start()

    spread = contract_last(weight.astype(BF16), onehot[...])
    row = lax.broadcasted_iota(jnp.int32, (group, 128), 0)
    lane = lax.broadcasted_iota(jnp.int32, (group, 128), 1)
    packed = jnp.zeros((group, 128), F32)
    for q in range(slots // 128):
        packed = jnp.where(row // 2 == q, spread[:, q * 128 : (q + 1) * 128], packed)
    packed = jnp.where(lane // cap == row % 2, packed, 0.0)
    packed = packed + pltpu.roll(packed, cap, 1)
    for e in range(group):
        w_send[e] = jnp.broadcast_to(packed[e : e + 1, :], (8, 128))
    w_recv[me] = w_send[me]

    def small_copy(source, target, sems, at, peer):
        return pltpu.make_async_remote_copy(
            src_ref=source.at[at],
            dst_ref=target.at[me],
            send_sem=sems.at[0],
            recv_sem=sems.at[1],
            device_id=peer,
            device_id_type=MESH,
        )

    def all_small(target, sems):
        return pltpu.make_async_remote_copy(
            src_ref=target.at[pl.ds(0, len(peers))],
            dst_ref=target.at[pl.ds(0, len(peers))],
            send_sem=sems.at[0],
            recv_sem=sems.at[1],
            device_id=peers[0],
            device_id_type=MESH,
        )

    for peer in peers:
        small_copy(w_send, w_recv, w_sem, peer[1], peer).start()

    mas_copy.wait()
    own_w[...] = mas[...].astype(BF16)
    far_copy = pltpu.make_async_remote_copy(
        src_ref=own_w, dst_ref=far_w, send_sem=y_ssem.at[0], recv_sem=y_rsem.at[0],
        device_id=(mirror, me), device_id_type=MESH,
    )
    far_copy.start()

    for p in range(1, len(PIECES)):
        tok_copies[p].wait()
        build(p)
        if p < len(PIECES) - 1:
            for peer in peers:
                row_copy(p, peer).start()
        else:
            for g, band in enumerate(bands):
                for peer in band:
                    row_copy(p, peer, p + g).start()

    hid_copy.wait()

    @pl.loop(0, slots // 256)
    def _(b):
        rows = pl.ds(pl.multiple_of(b * 256, 256), 256)
        hid_t[rows, :] = hid[:, rows].T

    all_small(w_recv, w_sem).wait_recv()
    lane8 = lax.broadcasted_iota(jnp.int32, (8, 128), 1)
    slot_w = jnp.concatenate(
        [jnp.where(lane8 < cap, w_recv[2 * q], w_recv[2 * q + 1]) for q in range(slots // 128)], 1
    )[0:1, :]

    @pl.loop(0, hid_n // 64)
    def _(b):
        rows = pl.ds(pl.multiple_of(b * 64, 64), 64)
        scaled[rows, :] = (hid[rows, :].astype(F32) * slot_w).astype(BF16)

    def project(p):
        kind, start, width = PIECES[p]
        matrix = own_w if kind == "own" else far_w
        base = start + (half if kind == "own" else 0)

        @pl.loop(0, slots // 256)
        def _(b):
            rows = pl.ds(pl.multiple_of(b * 256, 256), 256)
            v_buf[rows, base : base + width] = jnp.dot(
                hid_t[rows, :], matrix[:, start : start + width], preferred_element_type=F32
            )

    def add_score(p, first):
        kind, start, width = PIECES[p]
        base = start + (half if kind == "own" else 0)

        @pl.loop(0, slots // 64)
        def _(b):
            rows = pl.ds(pl.multiple_of(b * 64, 64), 64)
            product = recvs[p][rows, :].astype(F32) * v_buf[rows, base : base + width]
            partial = product[:, 0:128]
            for q in range(1, width // 128):
                partial = partial + product[:, q * 128 : (q + 1) * 128]
            if first:
                acc[rows, :] = partial
            else:
                acc[rows, :] = acc[rows, :] + partial

    def await_rows(p):
        all_rows(p).wait_recv()

    def grad_copy(p):
        kind, start, width = PIECES[p]
        return pltpu.make_async_remote_copy(
            src_ref=g_send.at[:, pl.ds(start, width)],
            dst_ref=g_recv.at[:, pl.ds(start, width)],
            send_sem=y_ssem.at[1 + p],
            recv_sem=y_rsem.at[1 + p],
            device_id=(mirror, me),
            device_id_type=MESH,
        )

    far = [p for p, piece in enumerate(PIECES) if piece[0] == "far"]
    own = [p for p, piece in enumerate(PIECES) if piece[0] == "own"]
    for p in own:
        project(p)
    for n, p in enumerate(far):
        kind, start, width = PIECES[p]
        await_rows(p)

        @pl.loop(0, hid_n // 256)
        def _(b):
            rows = pl.ds(pl.multiple_of(b * 256, 256), 256)
            g_send[rows, start : start + width] = jnp.dot(
                scaled[rows, :], recvs[p][...], preferred_element_type=F32
            ).astype(BF16)

        grad_copy(p).start()
        if n == 0:
            far_copy.wait_recv()
        project(p)
        add_score(p, n == 0)

    mom_copy.wait()
    sec_copy.wait()

    arrived = []

    def finish(p):
        kind, start, width = PIECES[p]
        for q in far:
            if q not in arrived and PIECES[q][1] < start + width:
                grad_copy(q).wait_recv()
                arrived.append(q)
        for c, n in blocks(0, width):
            fresh[:, :n] = jnp.dot(
                scaled[...], recvs[p][:, c : c + n], preferred_element_type=F32
            )

            @pl.loop(0, hid_n // 64)
            def _(b):
                rows = pl.ds(pl.multiple_of(b * 64, 64), 64)
                cols = slice(start + c, start + c + n)
                total = fresh[rows, :n] + g_recv[rows, cols].astype(F32)
                first_new = (beta_first / first_fix) * mom[rows, cols].astype(F32) + (
                    (1.0 - beta_first) / first_fix
                ) * total
                second_new = (beta_second / second_fix) * sec[rows, cols].astype(F32) + (
                    (1.0 - beta_second) / second_fix
                ) * (total * total)
                out[rows, cols] = (
                    first_new / (jnp.sqrt(second_new) + adam_eps) + decay_rate * mas[rows, cols]
                )

    for p in own[:-1]:
        await_rows(p)
        add_score(p, False)
        finish(p)

    last = own[-1]
    base, width = PIECES[last][1] + half, PIECES[last][2]

    def score_of(e):
        rows = pl.ds(pl.multiple_of(e * cap, cap), cap)
        product = recvs[last][rows, :].astype(F32) * v_buf[rows, base : base + width]
        total = acc[rows, :]
        for q in range(width // 128):
            total = total + product[:, q * 128 : (q + 1) * 128]
        line = contract_last(jnp.ones((8, 256), BF16), jnp.concatenate(split_two(total), 1))
        return jnp.concatenate([line, jnp.zeros((8, 128 - cap), F32)], 1)

    s_recv[me] = score_of(me)
    for g, band in enumerate(bands):
        all_rows(last, last + g, len(band)).wait_recv()
        for peer in band:
            s_send[peer[1]] = score_of(peer[1])
            small_copy(s_send, s_recv, s_sem, peer[1], peer).start()
    finish(last)

    all_small(s_recv, s_sem).wait_recv()
    got = jnp.concatenate([s_recv[e][0:1, :] for e in range(group)], 0)
    found = jnp.concatenate(
        [
            jnp.take_along_axis(got, jnp.maximum(rank[:, b * 128 : (b + 1) * 128], 0), axis=1)
            for b in range(toks_n // 128)
        ],
        1,
    )
    for k in range(ids.shape[0]):
        rg_ref[k : k + 1, :] = jnp.sum(
            jnp.where(ids[k : k + 1, :] == expert, found, 0.0), axis=0, keepdims=True
        )

    far_copy.wait_send()
    for p in far:
        grad_copy(p).wait_send()
    for p in range(len(PIECES) - 1):
        all_rows(p).wait_send()
    for g, band in enumerate(bands):
        all_rows(last, last + g, len(band)).wait_send()
    all_small(w_recv, w_sem).wait_send()
    all_small(s_recv, s_sem).wait_send()


def local(grad_out, router_weights, expert_ids, hidden, master, moment, second):
    toks_n, width = grad_out.shape[1:]
    hid_n, slots = hidden.shape[2:]
    half = master.shape[3]
    top = expert_ids.shape[2]
    pieces = len(PIECES)
    dma = pltpu.SemaphoreType.DMA
    hbm = pl.BlockSpec(memory_space=pl.ANY)
    vmem = pl.BlockSpec(memory_space=pltpu.VMEM)
    update, router = pl.pallas_call(
        kernel,
        out_shape=(
            pltpu.VMEM((hid_n, half), F32),
            pltpu.VMEM((top, toks_n), F32),
        ),
        in_specs=[vmem, vmem, hbm, hbm, hbm, hbm, hbm],
        out_specs=(vmem, vmem),
        scratch_shapes=[
            [pltpu.VMEM((toks_n, w), BF16) for _, _, w in PIECES],
            [pltpu.VMEM((slots, w), BF16) for _, _, w in PIECES],
            [pltpu.VMEM((slots, w), BF16) for _, _, w in PIECES],
            pltpu.VMEM((slots, toks_n), BF16),
            pltpu.VMEM((hid_n, slots), BF16),
            pltpu.VMEM((slots, hid_n), BF16),
            pltpu.VMEM((hid_n, slots), BF16),
            pltpu.VMEM((hid_n, half), F32),
            pltpu.VMEM((hid_n, half), BF16),
            pltpu.VMEM((hid_n, half), BF16),
            pltpu.VMEM((hid_n, half), BF16),
            pltpu.VMEM((hid_n, half), BF16),
            pltpu.VMEM((slots, width), F32),
            pltpu.VMEM((slots, 128), F32),
            pltpu.VMEM((hid_n, half), BF16),
            pltpu.VMEM((hid_n, half), BF16),
            pltpu.VMEM((hid_n, 256), F32),
            pltpu.VMEM((16, 8, 128), F32),
            pltpu.VMEM((16, 8, 128), F32),
            pltpu.VMEM((16, 8, 128), F32),
            pltpu.VMEM((16, 8, 128), F32),
            dma((pieces,)),
            dma((4,)),
            dma((pieces + len(GROUPS) - 1,)),
            dma((pieces + len(GROUPS) - 1,)),
            dma((2,)),
            dma((2,)),
            dma((1 + pieces,)),
            dma((1 + pieces,)),
        ],
        compiler_params=pltpu.CompilerParams(
            collective_id=0, has_side_effects=True, vmem_limit_bytes=58 << 20
        ),
    )(
        expert_ids[0].T, router_weights[0].T, grad_out[0], hidden[0, 0], master[0, 0],
        moment[0, 0], second[0, 0],
    )
    return (update[None, None], router.T[None])


def solution(mesh):
    placed = (
        P("section", "ep", None),
        P("section", "ep", None),
        P("section", "ep", None),
        P("section", "ep", None, None),
        P("section", "ep", None, None),
        P("section", "ep", None, None),
        P("section", "ep", None, None),
    )
    return jax.shard_map(
        local,
        mesh=mesh,
        in_specs=placed,
        out_specs=(P("section", "ep", None, None), P("section", "ep", None)),
        check_vma=False,
    )
```

```python
import functools

import jax
import jax.numpy as jnp
from jax import lax
from jax.experimental import pallas as pl
from jax.experimental.pallas import tpu as pltpu
from jax.sharding import PartitionSpec as P

beta_first = 0.9
beta_second = 0.95
adam_eps = 1e-08
decay_rate = 0.1
first_fix = 1.0 - 0.9**10
second_fix = 1.0 - 0.95**10

MESH = pl.DeviceIdType.MESH
F32 = jnp.float32
BF16 = jnp.bfloat16

PIECES = (("far", 0, 512), ("far", 512, 512), ("own", 0, 512), ("own", 512, 256), ("own", 768, 256))
GROUPS = ((4, 3, -3), (2, -2), (1, -1, 0))
ROUTES = ((4, 1), (3, 1), (-3, 1), (2, 1), (-2, 1), (1, 1), (-1, 1), (0, 1), (4, 0), (3, 0), (-3, 0), (2, 0), (-2, 0), (1, 0), (-1, 0))


def split_two(x):
    high = x.astype(BF16)
    return high, (x - high.astype(F32)).astype(BF16)


def blocks(start, width):
    return [(c, min(256, start + width - c)) for c in range(start, start + width, 256)]


def contract_last(a, b):
    return lax.dot_general(a, b, (((1,), (1,)), ((), ())), preferred_element_type=F32)


def kernel(
    ids_ref, rw_ref, tok_hbm, hid_hbm, mas_hbm, mom_hbm, sec_hbm, out, rg_ref,
    toks, sends, recvs, onehot, hid, hid_t, scaled, mas, mom, sec, own_w, far_w, v_buf, acc,
    g_send, g_recv, fresh, w_send, w_recv, s_send, s_recv,
    tok_sem, in_sem, row_ssem, row_rsem, w_sem, s_sem, y_ssem, y_rsem,
):
    group, cap = 16, 64
    toks_n = ids_ref.shape[1]
    hid_n, slots = hid.shape
    half = mas.shape[1]
    section = lax.axis_index("section")
    me = lax.axis_index("ep")
    count = lax.axis_size("section")
    mirror = lax.rem(section + count // 2, count)
    lower = (section < count // 2).astype(jnp.int32)
    offsets = {"far": lower * half, "own": (1 - lower) * half}
    z, xh = me // 2, me % 2

    tok_copies = []
    for p, (kind, start, width) in enumerate(PIECES):
        column = pl.multiple_of(offsets[kind] + start, 128)
        tok_copies.append(
            pltpu.make_async_copy(tok_hbm.at[:, pl.ds(column, width)], toks[p], tok_sem.at[p])
        )
    mas_copy = pltpu.make_async_copy(mas_hbm, mas, in_sem.at[0])
    hid_copy = pltpu.make_async_copy(hid_hbm, hid, in_sem.at[1])
    mom_copy = pltpu.make_async_copy(mom_hbm, mom, in_sem.at[2])
    sec_copy = pltpu.make_async_copy(sec_hbm, sec, in_sem.at[3])
    tok_copies[0].start()
    mas_copy.start()
    for copy in tok_copies[1:]:
        copy.start()
    hid_copy.start()
    mom_copy.start()
    sec_copy.start()

    peers = [
        (section, lax.rem(z + dz + 8, 8) * 2 + (lax.rem(xh + dx, 2))) for dz, dx in ROUTES
    ]
    bands = [
        [peer for (dz, _), peer in zip(ROUTES, peers) if dz in group_dz] for group_dz in GROUPS
    ]
    barrier = pltpu.get_barrier_semaphore()
    for peer in peers:
        pl.semaphore_signal(barrier, inc=1, device_id=peer, device_id_type=MESH)
    pl.semaphore_signal(barrier, inc=1, device_id=(mirror, me), device_id_type=MESH)

    ids = ids_ref[...]
    weights = rw_ref[...].astype(F32)
    expert = lax.broadcasted_iota(jnp.int32, (group, toks_n), 0)
    member = jnp.zeros((group, toks_n), F32)
    weight = jnp.zeros((group, toks_n), F32)
    for k in range(ids.shape[0]):
        named = ids[k : k + 1, :] == expert
        member = jnp.where(named, 1.0, member)
        weight = jnp.where(named, weights[k : k + 1, :], weight)
    parts = [member[:, b * 128 : (b + 1) * 128] for b in range(toks_n // 128)]
    column = lax.broadcasted_iota(jnp.int32, (128, 256), 1)
    before = (lax.broadcasted_iota(jnp.int32, (128, 256), 0) < column) | (column >= 128)
    counted = jnp.dot(
        jnp.concatenate(parts, 0).astype(BF16),
        jnp.where(before, 1.0, 0.0).astype(BF16),
        preferred_element_type=F32,
    )
    passed = jnp.zeros((group, 128), F32)
    ranks = []
    for b in range(toks_n // 128):
        rows = slice(b * group, (b + 1) * group)
        ranks.append(counted[rows, :128] + passed)
        passed = passed + counted[rows, 128:]
    rank = jnp.concatenate(ranks, 1).astype(jnp.int32)
    rank = jnp.where(member > 0.0, rank, -1)
    slot = lax.broadcasted_iota(jnp.int32, (cap, toks_n), 0)
    for e in range(group):
        onehot[e * cap : (e + 1) * cap, :] = jnp.where(
            rank[e : e + 1, :] == slot, 1.0, 0.0
        ).astype(BF16)

    def build(p):
        @pl.loop(0, slots // 256)
        def _(b):
            rows = pl.ds(pl.multiple_of(b * 256, 256), 256)
            sends[p][rows, :] = jnp.dot(
                onehot[rows, :], toks[p][...], preferred_element_type=F32
            ).astype(BF16)

        mine = pl.ds(pl.multiple_of(me * cap, cap), cap)
        recvs[p][mine, :] = sends[p][mine, :]

    def row_copy(p, peer, sem=None):
        sem = p if sem is None else sem
        there = pl.ds(pl.multiple_of(peer[1] * cap, cap), cap)
        mine = pl.ds(pl.multiple_of(me * cap, cap), cap)
        return pltpu.make_async_remote_copy(
            src_ref=sends[p].at[there, :],
            dst_ref=recvs[p].at[mine, :],
            send_sem=row_ssem.at[sem],
            recv_sem=row_rsem.at[sem],
            device_id=peer,
            device_id_type=MESH,
        )

    def all_rows(p, sem=None, number=None):
        sem = p if sem is None else sem
        rows = pl.ds(0, (len(peers) if number is None else number) * cap)
        return pltpu.make_async_remote_copy(
            src_ref=sends[p].at[rows, :],
            dst_ref=recvs[p].at[rows, :],
            send_sem=row_ssem.at[sem],
            recv_sem=row_rsem.at[sem],
            device_id=peers[0],
            device_id_type=MESH,
        )

    tok_copies[0].wait()
    build(0)
    pl.semaphore_wait(barrier, len(peers) + 1)
    for peer in peers:
        row_copy(0, peer).start()

    spread = contract_last(weight.astype(BF16), onehot[...])
    row = lax.broadcasted_iota(jnp.int32, (group, 128), 0)
    lane = lax.broadcasted_iota(jnp.int32, (group, 128), 1)
    packed = jnp.zeros((group, 128), F32)
    for q in range(slots // 128):
        packed = jnp.where(row // 2 == q, spread[:, q * 128 : (q + 1) * 128], packed)
    packed = jnp.where(lane // cap == row % 2, packed, 0.0)
    packed = packed + pltpu.roll(packed, cap, 1)
    for e in range(group):
        w_send[e] = jnp.broadcast_to(packed[e : e + 1, :], (8, 128))
    w_recv[me] = w_send[me]

    def small_copy(source, target, sems, at, peer):
        return pltpu.make_async_remote_copy(
            src_ref=source.at[at],
            dst_ref=target.at[me],
            send_sem=sems.at[0],
            recv_sem=sems.at[1],
            device_id=peer,
            device_id_type=MESH,
        )

    def all_small(target, sems):
        return pltpu.make_async_remote_copy(
            src_ref=target.at[pl.ds(0, len(peers))],
            dst_ref=target.at[pl.ds(0, len(peers))],
            send_sem=sems.at[0],
            recv_sem=sems.at[1],
            device_id=peers[0],
            device_id_type=MESH,
        )

    for peer in peers:
        small_copy(w_send, w_recv, w_sem, peer[1], peer).start()

    mas_copy.wait()
    own_w[...] = mas[...].astype(BF16)
    far_copy = pltpu.make_async_remote_copy(
        src_ref=own_w, dst_ref=far_w, send_sem=y_ssem.at[0], recv_sem=y_rsem.at[0],
        device_id=(mirror, me), device_id_type=MESH,
    )
    far_copy.start()

    for p in range(1, len(PIECES)):
        tok_copies[p].wait()
        build(p)
        if p < len(PIECES) - 1:
            for peer in peers:
                row_copy(p, peer).start()
        else:
            for g, band in enumerate(bands):
                for peer in band:
                    row_copy(p, peer, p + g).start()

    hid_copy.wait()

    @pl.loop(0, slots // 256)
    def _(b):
        rows = pl.ds(pl.multiple_of(b * 256, 256), 256)
        hid_t[rows, :] = hid[:, rows].T

    all_small(w_recv, w_sem).wait_recv()
    lane8 = lax.broadcasted_iota(jnp.int32, (8, 128), 1)
    slot_w = jnp.concatenate(
        [jnp.where(lane8 < cap, w_recv[2 * q], w_recv[2 * q + 1]) for q in range(slots // 128)], 1
    )[0:1, :]

    @pl.loop(0, hid_n // 64)
    def _(b):
        rows = pl.ds(pl.multiple_of(b * 64, 64), 64)
        scaled[rows, :] = (hid[rows, :].astype(F32) * slot_w).astype(BF16)

    def project(p):
        kind, start, width = PIECES[p]
        matrix = own_w if kind == "own" else far_w
        base = start + (half if kind == "own" else 0)

        @pl.loop(0, slots // 256)
        def _(b):
            rows = pl.ds(pl.multiple_of(b * 256, 256), 256)
            v_buf[rows, base : base + width] = jnp.dot(
                hid_t[rows, :], matrix[:, start : start + width], preferred_element_type=F32
            )

    def add_score(p, first):
        kind, start, width = PIECES[p]
        base = start + (half if kind == "own" else 0)

        @pl.loop(0, slots // 64)
        def _(b):
            rows = pl.ds(pl.multiple_of(b * 64, 64), 64)
            product = recvs[p][rows, :].astype(F32) * v_buf[rows, base : base + width]
            partial = product[:, 0:128]
            for q in range(1, width // 128):
                partial = partial + product[:, q * 128 : (q + 1) * 128]
            if first:
                acc[rows, :] = partial
            else:
                acc[rows, :] = acc[rows, :] + partial

    def await_rows(p):
        all_rows(p).wait_recv()

    def grad_copy(p):
        kind, start, width = PIECES[p]
        return pltpu.make_async_remote_copy(
            src_ref=g_send.at[:, pl.ds(start, width)],
            dst_ref=g_recv.at[:, pl.ds(start, width)],
            send_sem=y_ssem.at[1 + p],
            recv_sem=y_rsem.at[1 + p],
            device_id=(mirror, me),
            device_id_type=MESH,
        )

    far = [p for p, piece in enumerate(PIECES) if piece[0] == "far"]
    own = [p for p, piece in enumerate(PIECES) if piece[0] == "own"]
    for p in own:
        project(p)
    for n, p in enumerate(far):
        kind, start, width = PIECES[p]
        await_rows(p)

        @pl.loop(0, hid_n // 256)
        def _(b):
            rows = pl.ds(pl.multiple_of(b * 256, 256), 256)
            g_send[rows, start : start + width] = jnp.dot(
                scaled[rows, :], recvs[p][...], preferred_element_type=F32
            ).astype(BF16)

        grad_copy(p).start()
        if n == 0:
            far_copy.wait_recv()
        project(p)
        add_score(p, n == 0)

    mom_copy.wait()
    sec_copy.wait()

    arrived = []

    def finish(p):
        kind, start, width = PIECES[p]
        for q in far:
            if q not in arrived and PIECES[q][1] < start + width:
                grad_copy(q).wait_recv()
                arrived.append(q)
        for c, n in blocks(0, width):
            fresh[:, :n] = jnp.dot(
                scaled[...], recvs[p][:, c : c + n], preferred_element_type=F32
            )

            @pl.loop(0, hid_n // 64)
            def _(b):
                rows = pl.ds(pl.multiple_of(b * 64, 64), 64)
                cols = slice(start + c, start + c + n)
                total = fresh[rows, :n] + g_recv[rows, cols].astype(F32)
                first_new = (beta_first / first_fix) * mom[rows, cols].astype(F32) + (
                    (1.0 - beta_first) / first_fix
                ) * total
                second_new = (beta_second / second_fix) * sec[rows, cols].astype(F32) + (
                    (1.0 - beta_second) / second_fix
                ) * (total * total)
                out[rows, cols] = (
                    first_new / (jnp.sqrt(second_new) + adam_eps) + decay_rate * mas[rows, cols]
                )

    for p in own[:-1]:
        await_rows(p)
        add_score(p, False)
        finish(p)

    last = own[-1]
    base, width = PIECES[last][1] + half, PIECES[last][2]

    def score_of(e):
        rows = pl.ds(pl.multiple_of(e * cap, cap), cap)
        product = recvs[last][rows, :].astype(F32) * v_buf[rows, base : base + width]
        total = acc[rows, :]
        for q in range(width // 128):
            total = total + product[:, q * 128 : (q + 1) * 128]
        line = contract_last(jnp.ones((8, 256), BF16), jnp.concatenate(split_two(total), 1))
        return jnp.concatenate([line, jnp.zeros((8, 128 - cap), F32)], 1)

    s_recv[me] = score_of(me)
    for g, band in enumerate(bands):
        all_rows(last, last + g, len(band)).wait_recv()
        for peer in band:
            s_send[peer[1]] = score_of(peer[1])
            small_copy(s_send, s_recv, s_sem, peer[1], peer).start()
    finish(last)

    all_small(s_recv, s_sem).wait_recv()
    got = jnp.concatenate([s_recv[e][0:1, :] for e in range(group)], 0)
    found = jnp.concatenate(
        [
            jnp.take_along_axis(got, jnp.maximum(rank[:, b * 128 : (b + 1) * 128], 0), axis=1)
            for b in range(toks_n // 128)
        ],
        1,
    )
    for k in range(ids.shape[0]):
        rg_ref[k : k + 1, :] = jnp.sum(
            jnp.where(ids[k : k + 1, :] == expert, found, 0.0), axis=0, keepdims=True
        )

    far_copy.wait_send()
    for p in far:
        grad_copy(p).wait_send()
    for p in range(len(PIECES) - 1):
        all_rows(p).wait_send()
    for g, band in enumerate(bands):
        all_rows(last, last + g, len(band)).wait_send()
    all_small(w_recv, w_sem).wait_send()
    all_small(s_recv, s_sem).wait_send()


STORES = 6


def store(update_ref, router_ref, update_hbm, router_hbm, sem):
    copies = [pltpu.make_async_copy(router_ref, router_hbm, sem.at[STORES])]
    step = update_ref.shape[0] // STORES
    for i in range(STORES):
        rows = pl.ds(i * step, step)
        copies.append(
            pltpu.make_async_copy(update_ref.at[rows, :], update_hbm.at[rows, :], sem.at[i])
        )
    for copy in copies:
        copy.start()
    for copy in copies:
        copy.wait()


def local(grad_out, router_weights, expert_ids, hidden, master, moment, second):
    toks_n, width = grad_out.shape[1:]
    hid_n, slots = hidden.shape[2:]
    half = master.shape[3]
    top = expert_ids.shape[2]
    pieces = len(PIECES)
    dma = pltpu.SemaphoreType.DMA
    hbm = pl.BlockSpec(memory_space=pl.ANY)
    vmem = pl.BlockSpec(memory_space=pltpu.VMEM)
    update, router = pl.pallas_call(
        kernel,
        out_shape=(
            pltpu.VMEM((hid_n, half), F32),
            pltpu.VMEM((top, toks_n), F32),
        ),
        in_specs=[vmem, vmem, hbm, hbm, hbm, hbm, hbm],
        out_specs=(vmem, vmem),
        scratch_shapes=[
            [pltpu.VMEM((toks_n, w), BF16) for _, _, w in PIECES],
            [pltpu.VMEM((slots, w), BF16) for _, _, w in PIECES],
            [pltpu.VMEM((slots, w), BF16) for _, _, w in PIECES],
            pltpu.VMEM((slots, toks_n), BF16),
            pltpu.VMEM((hid_n, slots), BF16),
            pltpu.VMEM((slots, hid_n), BF16),
            pltpu.VMEM((hid_n, slots), BF16),
            pltpu.VMEM((hid_n, half), F32),
            pltpu.VMEM((hid_n, half), BF16),
            pltpu.VMEM((hid_n, half), BF16),
            pltpu.VMEM((hid_n, half), BF16),
            pltpu.VMEM((hid_n, half), BF16),
            pltpu.VMEM((slots, width), F32),
            pltpu.VMEM((slots, 128), F32),
            pltpu.VMEM((hid_n, half), BF16),
            pltpu.VMEM((hid_n, half), BF16),
            pltpu.VMEM((hid_n, 256), F32),
            pltpu.VMEM((16, 8, 128), F32),
            pltpu.VMEM((16, 8, 128), F32),
            pltpu.VMEM((16, 8, 128), F32),
            pltpu.VMEM((16, 8, 128), F32),
            dma((pieces,)),
            dma((4,)),
            dma((pieces + len(GROUPS) - 1,)),
            dma((pieces + len(GROUPS) - 1,)),
            dma((2,)),
            dma((2,)),
            dma((1 + pieces,)),
            dma((1 + pieces,)),
        ],
        compiler_params=pltpu.CompilerParams(
            collective_id=0, has_side_effects=True, vmem_limit_bytes=58 << 20
        ),
    )(
        expert_ids[0].T, router_weights[0].T, grad_out[0], hidden[0, 0], master[0, 0],
        moment[0, 0], second[0, 0],
    )
    update, router = pl.pallas_call(
        store,
        out_shape=(
            jax.ShapeDtypeStruct((hid_n, half), F32),
            jax.ShapeDtypeStruct((top, toks_n), F32),
        ),
        in_specs=[hbm, hbm],
        out_specs=(hbm, hbm),
        scratch_shapes=[dma((STORES + 1,))],
        compiler_params=pltpu.CompilerParams(vmem_limit_bytes=1 << 20),
    )(update, router)
    return (update[None, None], router.T[None])


def solution(mesh):
    placed = (
        P("section", "ep", None),
        P("section", "ep", None),
        P("section", "ep", None),
        P("section", "ep", None, None),
        P("section", "ep", None, None),
        P("section", "ep", None, None),
        P("section", "ep", None, None),
    )
    return jax.shard_map(
        local,
        mesh=mesh,
        in_specs=placed,
        out_specs=(P("section", "ep", None, None), P("section", "ep", None)),
        check_vma=False,
    )
```

```python
import functools

import jax
import jax.numpy as jnp
from jax import lax
from jax.experimental import pallas as pl
from jax.experimental.pallas import tpu as pltpu
from jax.sharding import PartitionSpec as P

beta_first = 0.9
beta_second = 0.95
adam_eps = 1e-08
decay_rate = 0.1
first_fix = 1.0 - 0.9**10
second_fix = 1.0 - 0.95**10

MESH = pl.DeviceIdType.MESH
F32 = jnp.float32
BF16 = jnp.bfloat16

PIECES = (("far", 0, 512), ("far", 512, 512), ("own", 0, 512), ("own", 512, 256), ("own", 768, 256))
GROUPS = ((6, 5), (4,), (3,), (2,), (1,))
ROUTES = ((4, 1), (3, 1), (-3, 1), (2, 1), (-2, 1), (1, 1), (-1, 1), (0, 1), (4, 0), (3, 0), (-3, 0), (2, 0), (-2, 0), (1, 0), (-1, 0))


def split_two(x):
    high = x.astype(BF16)
    return high, (x - high.astype(F32)).astype(BF16)


def blocks(start, width):
    return [(c, min(256, start + width - c)) for c in range(start, start + width, 256)]


def contract_last(a, b):
    return lax.dot_general(a, b, (((1,), (1,)), ((), ())), preferred_element_type=F32)


def kernel(
    ids_ref, rw_ref, tok_hbm, hid_hbm, mas_hbm, mom_hbm, sec_hbm, out, rg_ref,
    toks, sends, recvs, onehot, hid, hid_t, scaled, mas, mom, sec, own_w, far_w, v_buf, acc,
    g_send, g_recv, fresh, w_send, w_recv, s_send, s_recv,
    tok_sem, in_sem, row_ssem, row_rsem, w_sem, s_sem, y_ssem, y_rsem,
):
    group, cap = 16, 64
    toks_n = ids_ref.shape[1]
    hid_n, slots = hid.shape
    half = mas.shape[1]
    section = lax.axis_index("section")
    me = lax.axis_index("ep")
    count = lax.axis_size("section")
    mirror = lax.rem(section + count // 2, count)
    lower = (section < count // 2).astype(jnp.int32)
    offsets = {"far": lower * half, "own": (1 - lower) * half}
    z, xh = me // 2, me % 2

    tok_copies = []
    for p, (kind, start, width) in enumerate(PIECES):
        column = pl.multiple_of(offsets[kind] + start, 128)
        tok_copies.append(
            pltpu.make_async_copy(tok_hbm.at[:, pl.ds(column, width)], toks[p], tok_sem.at[p])
        )
    mas_copy = pltpu.make_async_copy(mas_hbm, mas, in_sem.at[0])
    hid_copy = pltpu.make_async_copy(hid_hbm, hid, in_sem.at[1])
    mom_copy = pltpu.make_async_copy(mom_hbm, mom, in_sem.at[2])
    sec_copy = pltpu.make_async_copy(sec_hbm, sec, in_sem.at[3])
    tok_copies[0].start()
    mas_copy.start()
    for copy in tok_copies[1:]:
        copy.start()
    hid_copy.start()
    mom_copy.start()
    sec_copy.start()

    peers = [
        (section, lax.rem(z + dz + 8, 8) * 2 + (lax.rem(xh + dx, 2))) for dz, dx in ROUTES
    ]
    bands = [
        [peer for (dz, dx), peer in zip(ROUTES, peers) if abs(dz) + 2 * dx in hops]
        for hops in GROUPS
    ]
    barrier = pltpu.get_barrier_semaphore()
    for peer in peers:
        pl.semaphore_signal(barrier, inc=1, device_id=peer, device_id_type=MESH)
    pl.semaphore_signal(barrier, inc=1, device_id=(mirror, me), device_id_type=MESH)

    ids = ids_ref[...]
    weights = rw_ref[...].astype(F32)
    expert = lax.broadcasted_iota(jnp.int32, (group, toks_n), 0)
    member = jnp.zeros((group, toks_n), F32)
    weight = jnp.zeros((group, toks_n), F32)
    for k in range(ids.shape[0]):
        named = ids[k : k + 1, :] == expert
        member = jnp.where(named, 1.0, member)
        weight = jnp.where(named, weights[k : k + 1, :], weight)
    parts = [member[:, b * 128 : (b + 1) * 128] for b in range(toks_n // 128)]
    column = lax.broadcasted_iota(jnp.int32, (128, 256), 1)
    before = (lax.broadcasted_iota(jnp.int32, (128, 256), 0) < column) | (column >= 128)
    counted = jnp.dot(
        jnp.concatenate(parts, 0).astype(BF16),
        jnp.where(before, 1.0, 0.0).astype(BF16),
        preferred_element_type=F32,
    )
    passed = jnp.zeros((group, 128), F32)
    ranks = []
    for b in range(toks_n // 128):
        rows = slice(b * group, (b + 1) * group)
        ranks.append(counted[rows, :128] + passed)
        passed = passed + counted[rows, 128:]
    rank = jnp.concatenate(ranks, 1).astype(jnp.int32)
    rank = jnp.where(member > 0.0, rank, -1)
    slot = lax.broadcasted_iota(jnp.int32, (cap, toks_n), 0)
    for e in range(group):
        onehot[e * cap : (e + 1) * cap, :] = jnp.where(
            rank[e : e + 1, :] == slot, 1.0, 0.0
        ).astype(BF16)

    def build(p):
        @pl.loop(0, slots // 256)
        def _(b):
            rows = pl.ds(pl.multiple_of(b * 256, 256), 256)
            sends[p][rows, :] = jnp.dot(
                onehot[rows, :], toks[p][...], preferred_element_type=F32
            ).astype(BF16)

        mine = pl.ds(pl.multiple_of(me * cap, cap), cap)
        recvs[p][mine, :] = sends[p][mine, :]

    def row_copy(p, peer, sem=None):
        sem = p if sem is None else sem
        there = pl.ds(pl.multiple_of(peer[1] * cap, cap), cap)
        mine = pl.ds(pl.multiple_of(me * cap, cap), cap)
        return pltpu.make_async_remote_copy(
            src_ref=sends[p].at[there, :],
            dst_ref=recvs[p].at[mine, :],
            send_sem=row_ssem.at[sem],
            recv_sem=row_rsem.at[sem],
            device_id=peer,
            device_id_type=MESH,
        )

    def all_rows(p, sem=None, number=None):
        sem = p if sem is None else sem
        rows = pl.ds(0, (len(peers) if number is None else number) * cap)
        return pltpu.make_async_remote_copy(
            src_ref=sends[p].at[rows, :],
            dst_ref=recvs[p].at[rows, :],
            send_sem=row_ssem.at[sem],
            recv_sem=row_rsem.at[sem],
            device_id=peers[0],
            device_id_type=MESH,
        )

    tok_copies[0].wait()
    build(0)
    pl.semaphore_wait(barrier, len(peers) + 1)
    for peer in peers:
        row_copy(0, peer).start()

    spread = contract_last(weight.astype(BF16), onehot[...])
    row = lax.broadcasted_iota(jnp.int32, (group, 128), 0)
    lane = lax.broadcasted_iota(jnp.int32, (group, 128), 1)
    packed = jnp.zeros((group, 128), F32)
    for q in range(slots // 128):
        packed = jnp.where(row // 2 == q, spread[:, q * 128 : (q + 1) * 128], packed)
    packed = jnp.where(lane // cap == row % 2, packed, 0.0)
    packed = packed + pltpu.roll(packed, cap, 1)
    for e in range(group):
        w_send[e] = jnp.broadcast_to(packed[e : e + 1, :], (8, 128))
    w_recv[me] = w_send[me]

    def small_copy(source, target, sems, at, peer):
        return pltpu.make_async_remote_copy(
            src_ref=source.at[at],
            dst_ref=target.at[me],
            send_sem=sems.at[0],
            recv_sem=sems.at[1],
            device_id=peer,
            device_id_type=MESH,
        )

    def all_small(target, sems):
        return pltpu.make_async_remote_copy(
            src_ref=target.at[pl.ds(0, len(peers))],
            dst_ref=target.at[pl.ds(0, len(peers))],
            send_sem=sems.at[0],
            recv_sem=sems.at[1],
            device_id=peers[0],
            device_id_type=MESH,
        )

    for peer in peers:
        small_copy(w_send, w_recv, w_sem, peer[1], peer).start()

    mas_copy.wait()
    own_w[...] = mas[...].astype(BF16)
    far_copy = pltpu.make_async_remote_copy(
        src_ref=own_w, dst_ref=far_w, send_sem=y_ssem.at[0], recv_sem=y_rsem.at[0],
        device_id=(mirror, me), device_id_type=MESH,
    )
    far_copy.start()

    for p in range(1, len(PIECES)):
        tok_copies[p].wait()
        build(p)
        if p < len(PIECES) - 1:
            for peer in peers:
                row_copy(p, peer).start()
        else:
            for g, band in enumerate(bands):
                for peer in band:
                    row_copy(p, peer, p + g).start()

    hid_copy.wait()

    @pl.loop(0, slots // 256)
    def _(b):
        rows = pl.ds(pl.multiple_of(b * 256, 256), 256)
        hid_t[rows, :] = hid[:, rows].T

    all_small(w_recv, w_sem).wait_recv()
    lane8 = lax.broadcasted_iota(jnp.int32, (8, 128), 1)
    slot_w = jnp.concatenate(
        [jnp.where(lane8 < cap, w_recv[2 * q], w_recv[2 * q + 1]) for q in range(slots // 128)], 1
    )[0:1, :]

    @pl.loop(0, hid_n // 64)
    def _(b):
        rows = pl.ds(pl.multiple_of(b * 64, 64), 64)
        scaled[rows, :] = (hid[rows, :].astype(F32) * slot_w).astype(BF16)

    def project(p):
        kind, start, width = PIECES[p]
        matrix = own_w if kind == "own" else far_w
        base = start + (half if kind == "own" else 0)

        @pl.loop(0, slots // 256)
        def _(b):
            rows = pl.ds(pl.multiple_of(b * 256, 256), 256)
            v_buf[rows, base : base + width] = jnp.dot(
                hid_t[rows, :], matrix[:, start : start + width], preferred_element_type=F32
            )

    def add_score(p, first):
        kind, start, width = PIECES[p]
        base = start + (half if kind == "own" else 0)

        @pl.loop(0, slots // 64)
        def _(b):
            rows = pl.ds(pl.multiple_of(b * 64, 64), 64)
            product = recvs[p][rows, :].astype(F32) * v_buf[rows, base : base + width]
            partial = product[:, 0:128]
            for q in range(1, width // 128):
                partial = partial + product[:, q * 128 : (q + 1) * 128]
            if first:
                acc[rows, :] = partial
            else:
                acc[rows, :] = acc[rows, :] + partial

    def await_rows(p):
        all_rows(p).wait_recv()

    def grad_copy(p):
        kind, start, width = PIECES[p]
        return pltpu.make_async_remote_copy(
            src_ref=g_send.at[:, pl.ds(start, width)],
            dst_ref=g_recv.at[:, pl.ds(start, width)],
            send_sem=y_ssem.at[1 + p],
            recv_sem=y_rsem.at[1 + p],
            device_id=(mirror, me),
            device_id_type=MESH,
        )

    far = [p for p, piece in enumerate(PIECES) if piece[0] == "far"]
    own = [p for p, piece in enumerate(PIECES) if piece[0] == "own"]
    for p in own:
        project(p)
    for n, p in enumerate(far):
        kind, start, width = PIECES[p]
        await_rows(p)

        @pl.loop(0, hid_n // 256)
        def _(b):
            rows = pl.ds(pl.multiple_of(b * 256, 256), 256)
            g_send[rows, start : start + width] = jnp.dot(
                scaled[rows, :], recvs[p][...], preferred_element_type=F32
            ).astype(BF16)

        grad_copy(p).start()
        if n == 0:
            far_copy.wait_recv()
        project(p)
        add_score(p, n == 0)

    mom_copy.wait()
    sec_copy.wait()

    arrived = []

    def finish(p):
        kind, start, width = PIECES[p]
        for q in far:
            if q not in arrived and PIECES[q][1] < start + width:
                grad_copy(q).wait_recv()
                arrived.append(q)
        for c, n in blocks(0, width):
            fresh[:, :n] = jnp.dot(
                scaled[...], recvs[p][:, c : c + n], preferred_element_type=F32
            )

            @pl.loop(0, hid_n // 64)
            def _(b):
                rows = pl.ds(pl.multiple_of(b * 64, 64), 64)
                cols = slice(start + c, start + c + n)
                total = fresh[rows, :n] + g_recv[rows, cols].astype(F32)
                first_new = (beta_first / first_fix) * mom[rows, cols].astype(F32) + (
                    (1.0 - beta_first) / first_fix
                ) * total
                second_new = (beta_second / second_fix) * sec[rows, cols].astype(F32) + (
                    (1.0 - beta_second) / second_fix
                ) * (total * total)
                out[rows, cols] = (
                    first_new / (jnp.sqrt(second_new) + adam_eps) + decay_rate * mas[rows, cols]
                )

    for p in own[:-1]:
        await_rows(p)
        add_score(p, False)
        finish(p)

    last = own[-1]
    base, width = PIECES[last][1] + half, PIECES[last][2]

    def score_of(e):
        rows = pl.ds(pl.multiple_of(e * cap, cap), cap)
        product = recvs[last][rows, :].astype(F32) * v_buf[rows, base : base + width]
        total = acc[rows, :]
        for q in range(width // 128):
            total = total + product[:, q * 128 : (q + 1) * 128]
        line = contract_last(jnp.ones((8, 256), BF16), jnp.concatenate(split_two(total), 1))
        return jnp.concatenate([line, jnp.zeros((8, 128 - cap), F32)], 1)


    for g, band in enumerate(bands):
        all_rows(last, last + g, len(band)).wait_recv()
        for peer in band:
            s_send[peer[1]] = score_of(peer[1])
            small_copy(s_send, s_recv, s_sem, peer[1], peer).start()
    s_recv[me] = score_of(me)
    finish(last)

    all_small(s_recv, s_sem).wait_recv()
    got = jnp.concatenate([s_recv[e][0:1, :] for e in range(group)], 0)
    found = jnp.concatenate(
        [
            jnp.take_along_axis(got, jnp.maximum(rank[:, b * 128 : (b + 1) * 128], 0), axis=1)
            for b in range(toks_n // 128)
        ],
        1,
    )
    for k in range(ids.shape[0]):
        rg_ref[k : k + 1, :] = jnp.sum(
            jnp.where(ids[k : k + 1, :] == expert, found, 0.0), axis=0, keepdims=True
        )

    far_copy.wait_send()
    for p in far:
        grad_copy(p).wait_send()
    for p in range(len(PIECES) - 1):
        all_rows(p).wait_send()
    for g, band in enumerate(bands):
        all_rows(last, last + g, len(band)).wait_send()
    all_small(w_recv, w_sem).wait_send()
    all_small(s_recv, s_sem).wait_send()


STORES = 6


def store(update_ref, router_ref, update_hbm, router_hbm, sem):
    copies = [pltpu.make_async_copy(router_ref, router_hbm, sem.at[STORES])]
    step = update_ref.shape[0] // STORES
    for i in range(STORES):
        rows = pl.ds(i * step, step)
        copies.append(
            pltpu.make_async_copy(update_ref.at[rows, :], update_hbm.at[rows, :], sem.at[i])
        )
    for copy in copies:
        copy.start()
    for copy in copies:
        copy.wait()


def local(grad_out, router_weights, expert_ids, hidden, master, moment, second):
    toks_n, width = grad_out.shape[1:]
    hid_n, slots = hidden.shape[2:]
    half = master.shape[3]
    top = expert_ids.shape[2]
    pieces = len(PIECES)
    dma = pltpu.SemaphoreType.DMA
    hbm = pl.BlockSpec(memory_space=pl.ANY)
    vmem = pl.BlockSpec(memory_space=pltpu.VMEM)
    update, router = pl.pallas_call(
        kernel,
        out_shape=(
            pltpu.VMEM((hid_n, half), F32),
            pltpu.VMEM((top, toks_n), F32),
        ),
        in_specs=[vmem, vmem, hbm, hbm, hbm, hbm, hbm],
        out_specs=(vmem, vmem),
        scratch_shapes=[
            [pltpu.VMEM((toks_n, w), BF16) for _, _, w in PIECES],
            [pltpu.VMEM((slots, w), BF16) for _, _, w in PIECES],
            [pltpu.VMEM((slots, w), BF16) for _, _, w in PIECES],
            pltpu.VMEM((slots, toks_n), BF16),
            pltpu.VMEM((hid_n, slots), BF16),
            pltpu.VMEM((slots, hid_n), BF16),
            pltpu.VMEM((hid_n, slots), BF16),
            pltpu.VMEM((hid_n, half), F32),
            pltpu.VMEM((hid_n, half), BF16),
            pltpu.VMEM((hid_n, half), BF16),
            pltpu.VMEM((hid_n, half), BF16),
            pltpu.VMEM((hid_n, half), BF16),
            pltpu.VMEM((slots, width), F32),
            pltpu.VMEM((slots, 128), F32),
            pltpu.VMEM((hid_n, half), BF16),
            pltpu.VMEM((hid_n, half), BF16),
            pltpu.VMEM((hid_n, 256), F32),
            pltpu.VMEM((16, 8, 128), F32),
            pltpu.VMEM((16, 8, 128), F32),
            pltpu.VMEM((16, 8, 128), F32),
            pltpu.VMEM((16, 8, 128), F32),
            dma((pieces,)),
            dma((4,)),
            dma((pieces + len(GROUPS) - 1,)),
            dma((pieces + len(GROUPS) - 1,)),
            dma((2,)),
            dma((2,)),
            dma((1 + pieces,)),
            dma((1 + pieces,)),
        ],
        compiler_params=pltpu.CompilerParams(
            collective_id=0, has_side_effects=True, vmem_limit_bytes=58 << 20
        ),
    )(
        expert_ids[0].T, router_weights[0].T, grad_out[0], hidden[0, 0], master[0, 0],
        moment[0, 0], second[0, 0],
    )
    update, router = pl.pallas_call(
        store,
        out_shape=(
            jax.ShapeDtypeStruct((hid_n, half), F32),
            jax.ShapeDtypeStruct((top, toks_n), F32),
        ),
        in_specs=[hbm, hbm],
        out_specs=(hbm, hbm),
        scratch_shapes=[dma((STORES + 1,))],
        compiler_params=pltpu.CompilerParams(vmem_limit_bytes=1 << 20),
    )(update, router)
    return (update[None, None], router.T[None])


def solution(mesh):
    placed = (
        P("section", "ep", None),
        P("section", "ep", None),
        P("section", "ep", None),
        P("section", "ep", None, None),
        P("section", "ep", None, None),
        P("section", "ep", None, None),
        P("section", "ep", None, None),
    )
    return jax.shard_map(
        local,
        mesh=mesh,
        in_specs=placed,
        out_specs=(P("section", "ep", None, None), P("section", "ep", None)),
        check_vma=False,
    )
```

```python
import functools

import jax
import jax.numpy as jnp
from jax import lax
from jax.experimental import pallas as pl
from jax.experimental.pallas import tpu as pltpu
from jax.sharding import PartitionSpec as P

beta_first = 0.9
beta_second = 0.95
adam_eps = 1e-08
decay_rate = 0.1
first_fix = 1.0 - 0.9**10
second_fix = 1.0 - 0.95**10

MESH = pl.DeviceIdType.MESH
F32 = jnp.float32
BF16 = jnp.bfloat16

PIECES = (("far", 0, 512), ("far", 512, 512), ("own", 0, 512), ("own", 512, 256), ("own", 768, 256))
GROUPS = ((6, 5), (4,), (3,), (2,), (1,))
ROUTES = ((4, 1), (3, 1), (-3, 1), (2, 1), (-2, 1), (1, 1), (-1, 1), (0, 1), (4, 0), (3, 0), (-3, 0), (2, 0), (-2, 0), (1, 0), (-1, 0))


def split_two(x):
    high = x.astype(BF16)
    return high, (x - high.astype(F32)).astype(BF16)


def blocks(start, width):
    return [(c, min(256, start + width - c)) for c in range(start, start + width, 256)]


def contract_last(a, b):
    return lax.dot_general(a, b, (((1,), (1,)), ((), ())), preferred_element_type=F32)


def kernel(
    ids_ref, rw_ref, tok_hbm, hid_hbm, mas_hbm, mom_hbm, sec_hbm, out, rg_ref,
    toks, sends, recvs, onehot, hid, hid_t, scaled, mas, mom, sec, own_w, far_w, v_buf, acc,
    g_send, g_recv, fresh, w_send, w_recv, s_send, s_recv,
    tok_sem, in_sem, row_ssem, row_rsem, w_sem, s_sem, y_ssem, y_rsem,
):
    group, cap = 16, 64
    toks_n = ids_ref.shape[1]
    hid_n, slots = hid.shape
    half = mas.shape[1]
    section = lax.axis_index("section")
    me = lax.axis_index("ep")
    count = lax.axis_size("section")
    mirror = lax.rem(section + count // 2, count)
    lower = (section < count // 2).astype(jnp.int32)
    offsets = {"far": lower * half, "own": (1 - lower) * half}
    z, xh = me // 2, me % 2

    tok_copies = []
    for p, (kind, start, width) in enumerate(PIECES):
        column = pl.multiple_of(offsets[kind] + start, 128)
        tok_copies.append(
            pltpu.make_async_copy(tok_hbm.at[:, pl.ds(column, width)], toks[p], tok_sem.at[p])
        )
    mas_copy = pltpu.make_async_copy(mas_hbm, mas, in_sem.at[0])
    hid_copy = pltpu.make_async_copy(hid_hbm, hid, in_sem.at[1])
    mom_copy = pltpu.make_async_copy(mom_hbm, mom, in_sem.at[2])
    sec_copy = pltpu.make_async_copy(sec_hbm, sec, in_sem.at[3])
    tok_copies[0].start()
    mas_copy.start()
    for copy in tok_copies[1:]:
        copy.start()
    hid_copy.start()
    mom_copy.start()
    sec_copy.start()

    peers = [
        (section, lax.rem(z + dz + 8, 8) * 2 + (lax.rem(xh + dx, 2))) for dz, dx in ROUTES
    ]
    bands = [
        [peer for (dz, dx), peer in zip(ROUTES, peers) if abs(dz) + 2 * dx in hops]
        for hops in GROUPS
    ]
    barrier = pltpu.get_barrier_semaphore()
    for peer in peers:
        pl.semaphore_signal(barrier, inc=1, device_id=peer, device_id_type=MESH)
    pl.semaphore_signal(barrier, inc=1, device_id=(mirror, me), device_id_type=MESH)

    ids = ids_ref[...]
    weights = rw_ref[...].astype(F32)
    expert = lax.broadcasted_iota(jnp.int32, (group, toks_n), 0)
    member = jnp.zeros((group, toks_n), F32)
    weight = jnp.zeros((group, toks_n), F32)
    for k in range(ids.shape[0]):
        named = ids[k : k + 1, :] == expert
        member = jnp.where(named, 1.0, member)
        weight = jnp.where(named, weights[k : k + 1, :], weight)
    parts = [member[:, b * 128 : (b + 1) * 128] for b in range(toks_n // 128)]
    column = lax.broadcasted_iota(jnp.int32, (128, 256), 1)
    before = (lax.broadcasted_iota(jnp.int32, (128, 256), 0) < column) | (column >= 128)
    counted = jnp.dot(
        jnp.concatenate(parts, 0).astype(BF16),
        jnp.where(before, 1.0, 0.0).astype(BF16),
        preferred_element_type=F32,
    )
    passed = jnp.zeros((group, 128), F32)
    ranks = []
    for b in range(toks_n // 128):
        rows = slice(b * group, (b + 1) * group)
        ranks.append(counted[rows, :128] + passed)
        passed = passed + counted[rows, 128:]
    rank = jnp.concatenate(ranks, 1).astype(jnp.int32)
    rank = jnp.where(member > 0.0, rank, -1)
    slot = lax.broadcasted_iota(jnp.int32, (cap, toks_n), 0)
    for e in range(group):
        onehot[e * cap : (e + 1) * cap, :] = jnp.where(
            rank[e : e + 1, :] == slot, 1.0, 0.0
        ).astype(BF16)

    def build(p):
        @pl.loop(0, slots // 256)
        def _(b):
            rows = pl.ds(pl.multiple_of(b * 256, 256), 256)
            sends[p][rows, :] = jnp.dot(
                onehot[rows, :], toks[p][...], preferred_element_type=F32
            ).astype(BF16)

        mine = pl.ds(pl.multiple_of(me * cap, cap), cap)
        recvs[p][mine, :] = sends[p][mine, :]

    def row_copy(p, peer, sem=None):
        sem = p if sem is None else sem
        there = pl.ds(pl.multiple_of(peer[1] * cap, cap), cap)
        mine = pl.ds(pl.multiple_of(me * cap, cap), cap)
        return pltpu.make_async_remote_copy(
            src_ref=sends[p].at[there, :],
            dst_ref=recvs[p].at[mine, :],
            send_sem=row_ssem.at[sem],
            recv_sem=row_rsem.at[sem],
            device_id=peer,
            device_id_type=MESH,
        )

    def all_rows(p, sem=None, number=None):
        sem = p if sem is None else sem
        rows = pl.ds(0, (len(peers) if number is None else number) * cap)
        return pltpu.make_async_remote_copy(
            src_ref=sends[p].at[rows, :],
            dst_ref=recvs[p].at[rows, :],
            send_sem=row_ssem.at[sem],
            recv_sem=row_rsem.at[sem],
            device_id=peers[0],
            device_id_type=MESH,
        )

    tok_copies[0].wait()
    build(0)
    pl.semaphore_wait(barrier, len(peers) + 1)
    for peer in peers:
        row_copy(0, peer).start()

    spread = contract_last(weight.astype(BF16), onehot[...])
    row = lax.broadcasted_iota(jnp.int32, (group, 128), 0)
    lane = lax.broadcasted_iota(jnp.int32, (group, 128), 1)
    packed = jnp.zeros((group, 128), F32)
    for q in range(slots // 128):
        packed = jnp.where(row // 2 == q, spread[:, q * 128 : (q + 1) * 128], packed)
    packed = jnp.where(lane // cap == row % 2, packed, 0.0)
    packed = packed + pltpu.roll(packed, cap, 1)
    for e in range(group):
        w_send[e] = jnp.broadcast_to(packed[e : e + 1, :], (8, 128))
    w_recv[me] = w_send[me]

    def small_copy(source, target, sems, at, peer):
        return pltpu.make_async_remote_copy(
            src_ref=source.at[at],
            dst_ref=target.at[me],
            send_sem=sems.at[0],
            recv_sem=sems.at[1],
            device_id=peer,
            device_id_type=MESH,
        )

    def all_small(target, sems):
        return pltpu.make_async_remote_copy(
            src_ref=target.at[pl.ds(0, len(peers))],
            dst_ref=target.at[pl.ds(0, len(peers))],
            send_sem=sems.at[0],
            recv_sem=sems.at[1],
            device_id=peers[0],
            device_id_type=MESH,
        )

    for peer in peers:
        small_copy(w_send, w_recv, w_sem, peer[1], peer).start()

    mas_copy.wait()
    own_w[...] = mas[...].astype(BF16)
    far_copy = pltpu.make_async_remote_copy(
        src_ref=own_w, dst_ref=far_w, send_sem=y_ssem.at[0], recv_sem=y_rsem.at[0],
        device_id=(mirror, me), device_id_type=MESH,
    )
    far_copy.start()

    for p in range(1, len(PIECES)):
        tok_copies[p].wait()
        build(p)
        if p < len(PIECES) - 1:
            for peer in peers:
                row_copy(p, peer).start()
        else:
            for g, band in enumerate(bands):
                for peer in band:
                    row_copy(p, peer, p + g).start()

    hid_copy.wait()

    @pl.loop(0, slots // 256)
    def _(b):
        rows = pl.ds(pl.multiple_of(b * 256, 256), 256)
        hid_t[rows, :] = hid[:, rows].T

    all_small(w_recv, w_sem).wait_recv()
    lane8 = lax.broadcasted_iota(jnp.int32, (8, 128), 1)
    slot_w = jnp.concatenate(
        [jnp.where(lane8 < cap, w_recv[2 * q], w_recv[2 * q + 1]) for q in range(slots // 128)], 1
    )[0:1, :]

    @pl.loop(0, hid_n // 64)
    def _(b):
        rows = pl.ds(pl.multiple_of(b * 64, 64), 64)
        scaled[rows, :] = (hid[rows, :].astype(F32) * slot_w).astype(BF16)

    def project(p):
        kind, start, width = PIECES[p]
        matrix = own_w if kind == "own" else far_w
        base = start + (half if kind == "own" else 0)

        @pl.loop(0, slots // 256)
        def _(b):
            rows = pl.ds(pl.multiple_of(b * 256, 256), 256)
            v_buf[rows, base : base + width] = jnp.dot(
                hid_t[rows, :], matrix[:, start : start + width], preferred_element_type=F32
            )

    def add_score(p, first):
        kind, start, width = PIECES[p]
        base = start + (half if kind == "own" else 0)

        @pl.loop(0, slots // 64)
        def _(b):
            rows = pl.ds(pl.multiple_of(b * 64, 64), 64)
            product = recvs[p][rows, :].astype(F32) * v_buf[rows, base : base + width]
            partial = product[:, 0:128]
            for q in range(1, width // 128):
                partial = partial + product[:, q * 128 : (q + 1) * 128]
            if first:
                acc[rows, :] = partial
            else:
                acc[rows, :] = acc[rows, :] + partial

    def await_rows(p):
        all_rows(p).wait_recv()

    def grad_copy(p):
        kind, start, width = PIECES[p]
        return pltpu.make_async_remote_copy(
            src_ref=g_send.at[:, pl.ds(start, width)],
            dst_ref=g_recv.at[:, pl.ds(start, width)],
            send_sem=y_ssem.at[1 + p],
            recv_sem=y_rsem.at[1 + p],
            device_id=(mirror, me),
            device_id_type=MESH,
        )

    far = [p for p, piece in enumerate(PIECES) if piece[0] == "far"]
    own = [p for p, piece in enumerate(PIECES) if piece[0] == "own"]
    for p in own:
        project(p)
    for n, p in enumerate(far):
        kind, start, width = PIECES[p]
        await_rows(p)

        @pl.loop(0, hid_n // 256)
        def _(b):
            rows = pl.ds(pl.multiple_of(b * 256, 256), 256)
            g_send[rows, start : start + width] = jnp.dot(
                scaled[rows, :], recvs[p][...], preferred_element_type=F32
            ).astype(BF16)

        grad_copy(p).start()
        if n == 0:
            far_copy.wait_recv()
        project(p)
        add_score(p, n == 0)

    mom_copy.wait()
    sec_copy.wait()

    arrived = []

    def finish(p):
        kind, start, width = PIECES[p]
        for q in far:
            if q not in arrived and PIECES[q][1] < start + width:
                grad_copy(q).wait_recv()
                arrived.append(q)
        for c, n in blocks(0, width):
            fresh[:, :n] = jnp.dot(
                scaled[...], recvs[p][:, c : c + n], preferred_element_type=F32
            )

            @pl.loop(0, hid_n // 64)
            def _(b):
                rows = pl.ds(pl.multiple_of(b * 64, 64), 64)
                cols = slice(start + c, start + c + n)
                total = fresh[rows, :n] + g_recv[rows, cols].astype(F32)
                first_new = (beta_first / first_fix) * mom[rows, cols].astype(F32) + (
                    (1.0 - beta_first) / first_fix
                ) * total
                second_new = (beta_second / second_fix) * sec[rows, cols].astype(F32) + (
                    (1.0 - beta_second) / second_fix
                ) * (total * total)
                out[rows, cols] = (
                    first_new / (jnp.sqrt(second_new) + adam_eps) + decay_rate * mas[rows, cols]
                )

    for p in own[:-1]:
        await_rows(p)
        add_score(p, False)
        finish(p)

    last = own[-1]
    base, width = PIECES[last][1] + half, PIECES[last][2]

    def score_of(e):
        rows = pl.ds(pl.multiple_of(e * cap, cap), cap)
        product = recvs[last][rows, :].astype(F32) * v_buf[rows, base : base + width]
        total = acc[rows, :]
        for q in range(width // 128):
            total = total + product[:, q * 128 : (q + 1) * 128]
        line = contract_last(jnp.ones((8, 256), BF16), jnp.concatenate(split_two(total), 1))
        return jnp.concatenate([line, jnp.zeros((8, 128 - cap), F32)], 1)[0:1, :]


    for g, band in enumerate(bands):
        all_rows(last, last + g, len(band)).wait_recv()
        for peer in band:
            s_send[peer[1]] = score_of(peer[1])
            small_copy(s_send, s_recv, s_sem, peer[1], peer).start()
    s_recv[me] = score_of(me)
    finish(last)

    all_small(s_recv, s_sem).wait_recv()
    got = jnp.concatenate([s_recv[e][0:1, :] for e in range(group)], 0)
    found = jnp.concatenate(
        [
            jnp.take_along_axis(got, jnp.maximum(rank[:, b * 128 : (b + 1) * 128], 0), axis=1)
            for b in range(toks_n // 128)
        ],
        1,
    )
    for k in range(ids.shape[0]):
        rg_ref[k : k + 1, :] = jnp.sum(
            jnp.where(ids[k : k + 1, :] == expert, found, 0.0), axis=0, keepdims=True
        )

    far_copy.wait_send()
    for p in far:
        grad_copy(p).wait_send()
    for p in range(len(PIECES) - 1):
        all_rows(p).wait_send()
    for g, band in enumerate(bands):
        all_rows(last, last + g, len(band)).wait_send()
    all_small(w_recv, w_sem).wait_send()
    all_small(s_recv, s_sem).wait_send()


STORES = 6


def store(update_ref, router_ref, update_hbm, router_hbm, sem):
    copies = [pltpu.make_async_copy(router_ref, router_hbm, sem.at[STORES])]
    step = update_ref.shape[0] // STORES
    for i in range(STORES):
        rows = pl.ds(i * step, step)
        copies.append(
            pltpu.make_async_copy(update_ref.at[rows, :], update_hbm.at[rows, :], sem.at[i])
        )
    for copy in copies:
        copy.start()
    for copy in copies:
        copy.wait()


def local(grad_out, router_weights, expert_ids, hidden, master, moment, second):
    toks_n, width = grad_out.shape[1:]
    hid_n, slots = hidden.shape[2:]
    half = master.shape[3]
    top = expert_ids.shape[2]
    pieces = len(PIECES)
    dma = pltpu.SemaphoreType.DMA
    hbm = pl.BlockSpec(memory_space=pl.ANY)
    vmem = pl.BlockSpec(memory_space=pltpu.VMEM)
    update, router = pl.pallas_call(
        kernel,
        out_shape=(
            pltpu.VMEM((hid_n, half), F32),
            pltpu.VMEM((top, toks_n), F32),
        ),
        in_specs=[vmem, vmem, hbm, hbm, hbm, hbm, hbm],
        out_specs=(vmem, vmem),
        scratch_shapes=[
            [pltpu.VMEM((toks_n, w), BF16) for _, _, w in PIECES],
            [pltpu.VMEM((slots, w), BF16) for _, _, w in PIECES],
            [pltpu.VMEM((slots, w), BF16) for _, _, w in PIECES],
            pltpu.VMEM((slots, toks_n), BF16),
            pltpu.VMEM((hid_n, slots), BF16),
            pltpu.VMEM((slots, hid_n), BF16),
            pltpu.VMEM((hid_n, slots), BF16),
            pltpu.VMEM((hid_n, half), F32),
            pltpu.VMEM((hid_n, half), BF16),
            pltpu.VMEM((hid_n, half), BF16),
            pltpu.VMEM((hid_n, half), BF16),
            pltpu.VMEM((hid_n, half), BF16),
            pltpu.VMEM((slots, width), F32),
            pltpu.VMEM((slots, 128), F32),
            pltpu.VMEM((hid_n, half), BF16),
            pltpu.VMEM((hid_n, half), BF16),
            pltpu.VMEM((hid_n, 256), F32),
            pltpu.VMEM((16, 8, 128), F32),
            pltpu.VMEM((16, 8, 128), F32),
            pltpu.VMEM((16, 1, 128), F32),
            pltpu.VMEM((16, 1, 128), F32),
            dma((pieces,)),
            dma((4,)),
            dma((pieces + len(GROUPS) - 1,)),
            dma((pieces + len(GROUPS) - 1,)),
            dma((2,)),
            dma((2,)),
            dma((1 + pieces,)),
            dma((1 + pieces,)),
        ],
        compiler_params=pltpu.CompilerParams(
            collective_id=0, has_side_effects=True, vmem_limit_bytes=58 << 20
        ),
    )(
        expert_ids[0].T, router_weights[0].T, grad_out[0], hidden[0, 0], master[0, 0],
        moment[0, 0], second[0, 0],
    )
    update, router = pl.pallas_call(
        store,
        out_shape=(
            jax.ShapeDtypeStruct((hid_n, half), F32),
            jax.ShapeDtypeStruct((top, toks_n), F32),
        ),
        in_specs=[hbm, hbm],
        out_specs=(hbm, hbm),
        scratch_shapes=[dma((STORES + 1,))],
        compiler_params=pltpu.CompilerParams(vmem_limit_bytes=1 << 20),
    )(update, router)
    return (update[None, None], router.T[None])


def solution(mesh):
    placed = (
        P("section", "ep", None),
        P("section", "ep", None),
        P("section", "ep", None),
        P("section", "ep", None, None),
        P("section", "ep", None, None),
        P("section", "ep", None, None),
        P("section", "ep", None, None),
    )
    return jax.shard_map(
        local,
        mesh=mesh,
        in_specs=placed,
        out_specs=(P("section", "ep", None, None), P("section", "ep", None)),
        check_vma=False,
    )
```
